128 devices in a mesh: row: 8 (over x, core), col: 16 (over z, y).
Axes of the slice: x: 4, y: 4, z: 4, core: 2. Of those that a mesh axis runs over, the one named last changes fastest.
Arguments:
- tiles: float32 [1024, 64, 64], P(('row', 'col')), may hold values from -6 to 6
- row_kernels: float32 [1024, 64, 64], P(('row', 'col')), may hold values from -0.2 to 1, as said below
- column_resample_kernels: float32 [1024, 64, 64], P(('row', 'col')), may hold values from -0.2 to 1, as said below
- destination: int32 [1024, 1], P(('row', 'col')), may hold values from 0 to 15; in each aligned block of 8 rows (0 to 7, 8 to 15, ...) no two rows name the same one
- row_offset: int32 [1024], P(('row', 'col')), may hold values from 0 to 64
- col_offset: int32 [1024], P(('row', 'col')), may hold values from 0 to 64
- exposure_weight: float32 [1024], P(('row', 'col')), may hold values from 0.2 to 5
- first_filter: float32 [32, 1, 3, 3], replicated, may hold values from -2 to 2
- first_bias: float32 [32], replicated, may hold values from -1.5 to 1.5
- second_filter: float32 [32, 32, 3, 3], replicated, may hold values from -0.375 to 0.375
- second_bias: float32 [32], replicated, may hold values from -1.5 to 1.5
- third_filter: float32 [32, 32, 3, 3], replicated, may hold values from -0.375 to 0.375
- third_bias: float32 [32], replicated, may hold values from -1.5 to 1.5
Outputs:
- features: float32 [32, 1024, 2048], P(None, 'row', 'col')
The draws below stay inside these ranges and needn't reach their ends.
Inputs may be any that keep to these rules, and one draw needn't show every extreme that they name: Among the tiles of one device at most 1 share a destination, and in every draw some device has exactly 1 tiles for one destination. `row_kernels`: entry (a, b) of a tile's matrix is the Lanczos-3 kernel sinc(x) sinc(x / 3) at x = b - a - s, zero where |x| >= 3, with one shift s of -0.5 to 0.5 for each tile. `column_resample_kernels`: entry (a, b) of a tile's matrix is the Lanczos-3 kernel sinc(x) sinc(x / 3) at x = b - a - s, zero where |x| >= 3, with one shift s of -0.5 to 0.5 for each tile.
All inputs are finite; a program needn't handle non-finite values.
Results may differ from the reference program's by a relative error of at most 0.0003.
Values sent between devices are 32-bit elements; how exact they have to be, the bound alone decides.
A program may use at most 128 MiB of HBM per device.

```python
import math
import jax
import jax.numpy as jnp
import numpy as np
from jax import lax

PS = 128
PATCH_ROWS_LOCAL = 1
TS = 64
EXP_DEV = 8
SLOTS = 1
CH = 32
TILES = 1024
NY = 1024
NX = 2048
N_COL = 16


def lanczos_table(key, count):
    shift = jax.random.uniform(key, (count, 1, 1), jnp.float32, -0.5, 0.5)
    place = jnp.arange(TS, dtype=jnp.float32)
    offset = place[None, None, :] - place[None, :, None] - shift
    value = jnp.sinc(offset) * jnp.sinc(offset / 3.0)
    return jnp.where(jnp.abs(offset) < 3.0, value, 0.0).astype(jnp.float32)


def draw_row_kernels(key, part):
    return lanczos_table(jax.random.fold_in(key, 11), TILES)


def draw_column_resample_kernels(key, part):
    return lanczos_table(jax.random.fold_in(key, 23), TILES)


def touch_ends(entries, stream_key, low, largest):
    longest = entries.shape.index(max(entries.shape))
    spots = []
    for shift in (0, 1):
        where = [jax.random.randint(jax.random.fold_in(stream_key, axis), (), 0, length) for axis, length in enumerate(entries.shape)]
        where[longest] = (where[longest] + shift) % entries.shape[longest]
        spots.append(tuple(where))
    return entries.at[spots[0]].set(low).at[spots[1]].set(largest)


def steps_of(rng, dims, split, low, top_value):
    gain, own = 1.0, jax.random.fold_in(rng, 6)
    for position, shards_of in split:
        draws = jnp.exp(jax.random.uniform(jax.random.fold_in(own, position), (shards_of,), jnp.float32, low / len(split), top_value / len(split)))
        gain = gain * jnp.repeat(draws, dims[position] // shards_of).reshape([-1 if axis == position else 1 for axis in range(len(dims))])
    return gain


def routed_block(key, own, number, rows, number_of, top, reach, skew):
    order = jax.random.permutation(key, number_of)
    packed, common = portions_of(number_of, rows * top, reach, skew, True), portions_of(number_of, rows * top, reach, skew, False)
    places = jnp.arange(number_of)

    def named(tallies, rotation):
        used = int((tallies > 0).sum())
        fixed = max(1, used // 4)
        shifted = fixed + (places - fixed + rotation * (used - fixed)) % max(1, number_of - fixed)
        return jnp.zeros((number_of,), jnp.int32).at[order[jnp.where(places < fixed, places, shifted)]].set(jnp.asarray(tallies, jnp.int32))

    tallies = jnp.where(number % 4 == 0, named(packed, number // 4), named(common, number - number // 4 - 1))
    mixed = jax.random.permutation(jax.random.fold_in(own, 3), number_of)
    giver, receiver = mixed[0:number_of // 2 * 2:2], mixed[1:number_of // 2 * 2:2]
    margin = jnp.minimum(tallies[giver] - 1, reach - tallies[receiver]) // 2
    margin = jnp.where((giver == order[0]) | (receiver == order[0]) | (tallies[receiver] == 0), 0, jnp.maximum(margin, 0))
    shifted = jax.random.randint(jax.random.fold_in(own, 4), (number_of // 2,), 0, 1 << 20) % (margin + 1)
    tallies = tallies.at[giver].add(-shifted).at[receiver].add(shifted)
    labels = jnp.searchsorted(jnp.cumsum(tallies), jnp.arange(rows * top), side="right").astype(jnp.int32)
    table = labels.reshape(top, rows).T
    table = table[jax.random.permutation(jax.random.fold_in(own, 1), rows)]
    rotation = jax.random.randint(jax.random.fold_in(own, 2), (rows, 1), 0, top)
    return jnp.take_along_axis(table, (jnp.arange(top)[None, :] + rotation) % top, axis=1)


def portions_of(amount, total, most, slope, full):
    loads = [(1 << 20) // math.isqrt(rank ** slope) + 1 for rank in range(1, amount + 1)]
    largest = most if full else min(most, max(-(-total // amount), total * loads[0] // sum(loads)))
    least = 1 if total - largest >= amount - 1 else 0
    counts, spare = [largest] + [least] * (amount - 1), total - largest - least * (amount - 1)
    while spare > 0:
        free = [i for i in range(1, amount) if counts[i] < largest] or [i for i in range(1, amount) if counts[i] < most]
        mass, remaining = sum([loads[i] for i in free]), spare
        for i in free:
            addition = min(most - counts[i], max(1, remaining * loads[i] // mass), spare)
            counts[i] = counts[i] + addition
            spare = spare - addition
    return np.array(counts)


def gaussian(own_key, shape, spread, most, split=(), kind=jnp.bfloat16):
    entries = jax.random.normal(own_key, shape, jnp.float32) * spread
    if len(split) > 0:
        entries = steps_of(own_key, shape, split, -0.22, 0.18) * entries
    return jnp.clip(entries, min=-most, max=most).astype(kind)


def setup_inputs(seed: int = 0) -> dict:
    seeds = jax.random.split(jax.random.key(seed), 14)
    tiles = gaussian(seeds[0], (TILES, TS, TS), 1.0, 6.0, ((0, 128),), jnp.float32)
    row_kernels = draw_row_kernels(jax.random.fold_in(seeds[13], 71), 0)
    column_resample_kernels = draw_column_resample_kernels(jax.random.fold_in(seeds[13], 71), 0)
    destination_keys = jax.random.split(jax.random.fold_in(seeds[3], 1), TILES // EXP_DEV)
    destination_turns = jax.random.permutation(jax.random.fold_in(seeds[3], 3), TILES // EXP_DEV)
    destination = jax.vmap(lambda own, number: routed_block(jax.random.fold_in(seeds[3], 2), own, number, EXP_DEV, N_COL, 1, SLOTS, 2))(destination_keys, destination_turns).reshape((TILES, 1))
    row_offset = touch_ends(jax.random.randint(seeds[4], (TILES,), 0, PATCH_ROWS_LOCAL * PS - TS + 1), jax.random.fold_in(seeds[4], 1), 0, PATCH_ROWS_LOCAL * PS - TS).astype(jnp.int32)
    col_offset = touch_ends(jax.random.randint(seeds[5], (TILES,), 0, PS - TS + 1), jax.random.fold_in(seeds[5], 1), 0, PS - TS).astype(jnp.int32)
    exposure_weight = jnp.clip(jnp.exp(math.log(5.0) - 3.218876 * jax.random.uniform(seeds[6], (TILES,), jnp.float32) ** steps_of(seeds[6], (TILES,), ((0, 128),), -0.2, 0.2)), 0.2, 5.0)
    first_filter = gaussian(seeds[7], (CH, 1, 3, 3), 9 ** -0.5, 2.0, (), jnp.float32)
    first_bias = gaussian(seeds[8], (CH,), 0.3, 1.5, (), jnp.float32)
    second_filter = gaussian(seeds[9], (CH, CH, 3, 3), (9 * CH) ** -0.5, 0.375, (), jnp.float32)
    second_bias = gaussian(seeds[10], (CH,), 0.3, 1.5, (), jnp.float32)
    third_filter = gaussian(seeds[11], (CH, CH, 3, 3), (9 * CH) ** -0.5, 0.375, (), jnp.float32)
    third_bias = gaussian(seeds[12], (CH,), 0.3, 1.5, (), jnp.float32)
    return {"tiles": tiles, "row_kernels": row_kernels, "column_resample_kernels": column_resample_kernels, "destination": destination, "row_offset": row_offset, "col_offset": col_offset, "exposure_weight": exposure_weight, "first_filter": first_filter, "first_bias": first_bias, "second_filter": second_filter, "second_bias": second_bias, "third_filter": third_filter, "third_bias": third_bias}


def resample_all(kernel_rows, images, kernel_column_slice):
    middle_activation = jnp.einsum('iab,ibc->iac', kernel_rows, images, precision=lax.Precision.HIGHEST)
    return jnp.einsum('wbz,wuz->wbu', middle_activation, kernel_column_slice, precision=lax.Precision.HIGHEST)


def dilated(field, conv_kernel_matrix, spacing):
    out = lax.conv_general_dilated(field[None], conv_kernel_matrix, (1, 1), ((spacing, spacing), (spacing, spacing)),
                                   rhs_dilation=(spacing, spacing), dimension_numbers=('NCHW', 'OIHW', 'NCHW'),
                                   precision=lax.Precision.HIGHEST)
    return out[0]


def reference(tiles, row_kernels, column_resample_kernels, destination, row_offset, col_offset, exposure_weight,
              first_filter, first_bias, second_filter, second_bias, third_filter, third_bias):
    resampled = resample_all(row_kernels, tiles, column_resample_kernels)
    target_patch = destination[:, 0].astype(jnp.int32)
    holder_row = jnp.arange(TILES, dtype=jnp.int32) // (EXP_DEV * N_COL)
    top = holder_row * (PATCH_ROWS_LOCAL * PS) + row_offset.astype(jnp.int32)
    left = target_patch * PS + col_offset.astype(jnp.int32)
    ones = jnp.ones((TS, TS), jnp.float32)

    def add_tile(carry, item):
        numer, cover = carry
        image, weight, ypos, xpos = item
        ypos = ypos.astype(jnp.int32)
        xpos = xpos.astype(jnp.int32)
        old = lax.dynamic_slice(numer, (ypos, xpos), (TS, TS))
        numer = lax.dynamic_update_slice(numer, old + weight * image, (ypos, xpos))
        old_cover = lax.dynamic_slice(cover, (ypos, xpos), (TS, TS))
        cover = lax.dynamic_update_slice(cover, old_cover + weight * ones, (ypos, xpos))
        return (numer, cover), None

    start = (jnp.zeros((NY, NX), jnp.float32), jnp.zeros((NY, NX), jnp.float32))
    (numer, cover), _ = lax.scan(add_tile, start, (resampled, exposure_weight, top, left))
    coadd = numer / (1.0 + cover)
    first = jax.nn.relu(dilated(coadd[None], first_filter, 1) + first_bias[:, None, None])
    second = jax.nn.relu(dilated(first, second_filter, 2) + second_bias[:, None, None])
    return dilated(second, third_filter, 4) + third_bias[:, None, None]
```

```python
import functools
import jax
import jax.numpy as jnp
from jax import lax
from jax.experimental import pallas as pl
from jax.experimental.pallas import tpu as pltpu
from jax.sharding import PartitionSpec as P

BF = jnp.bfloat16
F32 = jnp.float32


def split(x):
    hi = x.astype(BF)
    return hi, (x - hi.astype(F32)).astype(BF)


def build_weights(f1_ref, b1_ref, f2_ref, f3_ref, w1_ref, w2_ref, w3_ref):
    for f_ref, w_ref in ((f2_ref, w2_ref), (f3_ref, w3_ref)):
        for dx in range(3):
            row = jnp.concatenate(
                [f_ref[dy * 3 + dx] for dy in range(3)] + [jnp.zeros((32, 160), F32)], axis=1)
            for yo in range(6):
                moved = row if yo == 0 else pltpu.roll(row, 32 * yo, 1)
                hi, lo = split(moved)
                w_ref[0, dx, yo * 32:(yo + 1) * 32, :] = hi
                w_ref[1, dx, yo * 32:(yo + 1) * 32, :] = lo
    f1 = f1_ref[...]
    hi, lo = split(f1)
    hi = hi.astype(F32)
    lo = lo.astype(F32)
    b = b1_ref[...]
    bhi, blo = split(b)
    lane = lax.broadcasted_iota(jnp.int32, (32, 256), 1)
    for yo in range(8):
        acc = jnp.where(lane == 144, bhi.astype(F32), 0.0) + jnp.where(lane == 145, blo.astype(F32), 0.0)
        for part, w in enumerate((hi, hi, lo)):
            for dx in range(3):
                for dy in range(3):
                    acc = acc + jnp.where(lane == part * 48 + dx * 16 + yo + dy, w[:, dy * 3 + dx:dy * 3 + dx + 1], 0.0)
        r = (yo % 2) * 128 + (yo // 2) * 32
        w1_ref[r:r + 32, :] = acc.astype(BF)


def conv_body(row, col, p_ref, w1_ref, w2_ref, w3_ref, b2_ref, b3_ref, out_ref,
              ps, f_hi, f_lo, s_hi, s_lo):
    p = p_ref[...]
    ps[0] = pltpu.roll(p, 1, 1)
    ps[1] = p
    ps[2] = pltpu.roll(p, 255, 1)
    lane = lax.broadcasted_iota(jnp.int32, (1, 256), 1)
    dead = jnp.logical_or(jnp.logical_and(col == 0, lane >= 192),
                          jnp.logical_and(col == 15, jnp.logical_and(lane >= 128, lane < 192)))
    cmask = jnp.where(dead, 0.0, 1.0)
    sub = lax.broadcasted_iota(jnp.int32, (16, 256), 0)
    ones = jnp.where(sub < 2, 1.0, 0.0).astype(BF)
    pad = jnp.zeros((96, 256), BF)
    w1 = w1_ref[...]
    n_rows = 1024
    base = row * 128

    def valid(y):
        yy = base + y
        return jnp.where(jnp.logical_and(yy >= 0, yy < n_rows), 1.0, 0.0)

    @pl.loop(0, 18)
    def _(g):
        hs, ls = [], []
        for dx in range(3):
            h, l = split(ps[dx, pl.ds(pl.multiple_of(8 * g, 8), 16), :])
            hs.append(h)
            ls.append(l)
        rhs = jnp.concatenate(hs + ls + hs + [ones, pad], axis=0)
        acc = jnp.dot(w1, rhs, preferred_element_type=F32)
        for q in range(2):
            for m in range(4):
                mask = cmask * valid(8 * g + 2 * m + q - 6)
                v = jnp.maximum(acc[q * 128 + m * 32:q * 128 + m * 32 + 32, :], 0.0) * mask
                h, l = split(v)
                at = pl.ds(pl.multiple_of((4 * g + m) * 32, 32), 32)
                f_hi[q, at, :] = h
                f_lo[q, at, :] = l

    b2 = b2_ref[...]

    @pl.loop(0, 24)
    def _(t):
        q = lax.rem(t, 2)
        m0 = jnp.minimum(6 * (t // 2), 62)
        at = pl.ds(pl.multiple_of(32 * m0, 64), 256)
        hi = f_hi[q, at, :]
        lo = f_lo[q, at, :]
        parts = []
        for dx in range(3):
            parts.append(jnp.dot(w2_ref[0, dx], hi, preferred_element_type=F32)
                         + jnp.dot(w2_ref[1, dx], hi, preferred_element_type=F32)
                         + jnp.dot(w2_ref[0, dx], lo, preferred_element_type=F32))
        acc = parts[1] + pltpu.roll(parts[0], 2, 1) + pltpu.roll(parts[2], 254, 1)
        n0 = m0 // 2
        for yo in range(6):
            mask = cmask * valid(2 * (m0 + yo) + q - 4)
            v = acc[yo * 32:yo * 32 + 32, :]
            v = jnp.maximum(v + b2, 0.0) * mask
            r = 2 * (yo % 2) + q
            at = pl.ds(pl.multiple_of((n0 + yo // 2) * 32, 32), 32)
            for k, sh in enumerate((pltpu.roll(v, 4, 1), v, pltpu.roll(v, 252, 1))):
                h, l = split(sh[:, :128])
                s_hi[k, r, at, :] = h
                s_lo[k, r, at, :] = l

    b3 = b3_ref[...][:, :128]

    @pl.loop(0, 12)
    def _(t):
        half = lax.rem(t, 2)
        n0 = jnp.minimum(6 * (t // 2), 26)
        at = pl.ds(pl.multiple_of(32 * n0, 64), 256)
        acc = None
        for dx in range(3):
            hi = jnp.concatenate([s_hi[dx, 2 * half, at, :], s_hi[dx, 2 * half + 1, at, :]], axis=1)
            lo = jnp.concatenate([s_lo[dx, 2 * half, at, :], s_lo[dx, 2 * half + 1, at, :]], axis=1)
            part = (jnp.dot(w3_ref[0, dx], hi, preferred_element_type=F32)
                    + jnp.dot(w3_ref[1, dx], hi, preferred_element_type=F32)
                    + jnp.dot(w3_ref[0, dx], lo, preferred_element_type=F32))
            acc = part if acc is None else acc + part
        for e in range(2):
            for yo in range(6):
                v = acc[yo * 32:yo * 32 + 32, e * 128:e * 128 + 128] + b3
                y = 4 * (n0 + yo) + 2 * half + e
                for k in range(4):
                    out_ref[pl.ds(k * 1024 + y, 8, stride=128), :] = v[8 * k:8 * k + 8, :]


def conv_kernel(*refs):
    conv_body(lax.axis_index("row"), lax.axis_index("col"), *refs)


W_SHAPES = [jax.ShapeDtypeStruct((256, 256), BF), jax.ShapeDtypeStruct((2, 3, 192, 256), BF),
            jax.ShapeDtypeStruct((2, 3, 192, 256), BF)]


def conv_call(p, w1, w2, w3, b2, b3):
    vm = pl.BlockSpec(memory_space=pltpu.VMEM)
    return pl.pallas_call(
        conv_kernel,
        out_shape=jax.ShapeDtypeStruct((4096, 128), F32),
        in_specs=[vm] * 6,
        out_specs=vm,
        scratch_shapes=[pltpu.VMEM((3, 152, 256), F32),
                        pltpu.VMEM((2, 74 * 32, 256), BF), pltpu.VMEM((2, 74 * 32, 256), BF),
                        pltpu.VMEM((3, 4, 34 * 32, 128), BF), pltpu.VMEM((3, 4, 34 * 32, 128), BF)],
        compiler_params=pltpu.CompilerParams(vmem_limit_bytes=48 << 20),
        name="convs",
    )(p, w1, w2, w3, b2, b3)


N_ROW = 8
N_COL = 16
TILES_DEV = 8
TS = 64
MESH = pl.DeviceIdType.MESH


def dot3(ah, al, bh, bl, dims):
    d = functools.partial(lax.dot_general, dimension_numbers=(dims, ((), ())), preferred_element_type=F32)
    return d(ah, bh) + d(al, bh) + d(ah, bl)


def comm_kernel(dest, roff, coff, wgt, tiles, rker, cker, f1_ref, b1_ref, f2_ref, f3_ref,
                p_ref, w1_ref, w2_ref, w3_ref,
                ckpad, packed, send, recv, spread, edge_out, edge_in,
                send_sem, recv_sem, esend_sem, erecv_sem):
    row = lax.axis_index("row")
    col = lax.axis_index("col")
    up = lax.rem(row + N_ROW - 1, N_ROW)
    down = lax.rem(row + 1, N_ROW)
    left = lax.rem(col + N_COL - 1, N_COL)
    right = lax.rem(col + 1, N_COL)

    barrier = pltpu.get_barrier_semaphore()

    @pl.loop(1, N_COL)
    def _(k):
        pl.semaphore_signal(barrier, inc=1, device_id=(row, lax.rem(col + k, N_COL)), device_id_type=MESH)

    for r in (up, down):
        for c in (left, col, right):
            pl.semaphore_signal(barrier, inc=1, device_id=(r, c), device_id_type=MESH)

    ckpad[...] = jnp.zeros_like(ckpad)

    @pl.loop(0, TILES_DEV)
    def _(t):
        rh, rl = split(rker[t])
        th, tl = split(tiles[t])
        mid = dot3(rh, rl, th, tl, ((1,), (0,)))
        ckpad[TS:2 * TS, :] = cker[t]
        placed = ckpad[pl.ds(TS - coff[t], 2 * TS), :]
        mh, ml = split(mid)
        ch, cl = split(placed)
        img = dot3(mh, ml, ch, cl, ((1,), (1,)))
        packed[t] = img[:32, :] + pltpu.roll(img[32:, :], 64, 1)

    sub8 = lax.broadcasted_iota(jnp.int32, (8, 128), 0)

    @pl.loop(0, N_COL)
    def _(c):
        acc = None
        ro = jnp.float32(0.0)
        co = jnp.float32(0.0)
        w = jnp.float32(0.0)
        for t in range(TILES_DEV):
            hit = jnp.where(dest[t] == c, 1.0, 0.0)
            wt = hit * wgt[t]
            ro = ro + hit * roff[t].astype(F32)
            co = co + hit * coff[t].astype(F32)
            w = w + wt
            term = packed[t] * wt
            acc = term if acc is None else acc + term
        send[c, 0:32, :] = acc
        send[c, 32:40, :] = jnp.where(sub8 == 0, ro, jnp.where(sub8 == 1, co, w))

    pl.semaphore_wait(barrier, N_COL - 1 + 6)

    def tile_copy(k):
        c = lax.rem(col + k, N_COL)
        return pltpu.make_async_remote_copy(
            src_ref=send.at[c], dst_ref=recv.at[k], send_sem=send_sem.at[k], recv_sem=recv_sem.at[k],
            device_id=(row, c), device_id_type=MESH)

    @pl.loop(1, N_COL)
    def _(k):
        tile_copy(k).start()

    recv[0] = send[col]
    build_weights(f1_ref, b1_ref, f2_ref, f3_ref, w1_ref, w2_ref, w3_ref)

    @pl.loop(1, N_COL)
    def _(k):
        tile_copy(k).wait()

    lane = lax.broadcasted_iota(jnp.int32, (1, 128), 1).astype(F32)
    suby = lax.broadcasted_iota(jnp.int32, (128, 128), 0).astype(F32)
    lanes = lax.broadcasted_iota(jnp.int32, (128, 128), 1)
    lane_a = (lanes % TS).astype(F32)
    cover = jnp.zeros((128, 128), F32)
    numer = jnp.zeros((128, 256), F32)
    for pair in range(N_COL // 2):
        ros = []
        for e in range(2):
            s = 2 * pair + e
            pk = recv[s, 0:32, :]
            ro = recv[s, 32:33, :]
            co = recv[s, 33:34, :]
            w = recv[s, 34:35, :]
            at = lane - co
            inside = jnp.logical_and(at >= 0.0, at < float(TS))
            a = jnp.where(inside, pk, 0.0)
            b = jnp.where(inside, pltpu.roll(pk, 64, 1), 0.0)
            for half, v in enumerate((a, b)):
                h, l = split(v)
                r = s * TS + half * 32
                spread[r:r + 32, 0:128] = h
                spread[r:r + 32, 128:256] = l
            wcol = jnp.where(inside, w, 0.0)
            dy = suby - ro
            cover = cover + jnp.where(jnp.logical_and(dy >= 0.0, dy < float(TS)), wcol, 0.0)
            ros.append(ro)
        want = jnp.where(lanes < TS, ros[0], ros[1]) + lane_a
        pick = jnp.where(suby == want, 1.0, 0.0).astype(BF)
        numer = numer + jnp.dot(pick, spread[pair * 128:pair * 128 + 128, :], preferred_element_type=F32)
    coadd = (numer[:, :128] + numer[:, 128:]) / (1.0 + cover)

    edge_out[0] = coadd[0:8, :]
    edge_out[1] = coadd[120:128, :]
    lane8 = lax.broadcasted_iota(jnp.int32, (8, 128), 1)
    lcols = jnp.zeros((8, 128), F32)
    rcols = jnp.zeros((8, 128), F32)
    for k in range(16):
        blk = coadd[8 * k:8 * k + 8, :]
        here = jnp.logical_and(lane8 >= 8 * k, lane8 < 8 * k + 8)
        lcols = jnp.where(here, blk if k == 0 else pltpu.roll(blk, 8 * k, 1), lcols)
        rcols = jnp.where(here, blk if k == 15 else pltpu.roll(blk, 8 * k + 8, 1), rcols)
    edge_out[2] = lcols
    edge_out[3] = rcols
    plan = ((0, 1, (down, col)), (1, 0, (up, col)), (2, 3, (row, right)), (3, 2, (row, left)),
            (4, 1, (down, right)), (5, 1, (down, left)), (6, 0, (up, right)), (7, 0, (up, left)))
    copies = [pltpu.make_async_remote_copy(
        src_ref=edge_out.at[src], dst_ref=edge_in.at[slot], send_sem=esend_sem.at[slot],
        recv_sem=erecv_sem.at[slot], device_id=dev, device_id_type=MESH) for slot, src, dev in plan]
    for c in copies:
        c.start()
    p_ref[...] = jnp.zeros_like(p_ref)
    p_ref[7:135, 0:128] = coadd
    for c in copies:
        c.wait()

    has_up = jnp.where(row > 0, 1.0, 0.0)
    has_down = jnp.where(row < N_ROW - 1, 1.0, 0.0)
    has_left = jnp.where(col > 0, 1.0, 0.0)
    has_right = jnp.where(col < N_COL - 1, 1.0, 0.0)
    side = jnp.where(lane8 < TS, has_right, has_left)
    p_ref[0:7, 0:128] = edge_in[0][1:8, :] * has_up
    p_ref[135:142, 0:128] = edge_in[1][0:7, :] * has_down
    p_ref[0:7, 128:256] = (jnp.where(lane8 < TS, edge_in[5], edge_in[4]) * side * has_up)[1:8, :]
    p_ref[135:142, 128:256] = (jnp.where(lane8 < TS, edge_in[7], edge_in[6]) * side * has_down)[0:7, :]
    from_left = edge_in[2]
    from_right = edge_in[3]
    for k in range(16):
        r = from_right if k == 0 else pltpu.roll(from_right, 128 - 8 * k, 1)
        l = from_left if k == 15 else pltpu.roll(from_left, 120 - 8 * k, 1)
        p_ref[7 + 8 * k:15 + 8 * k, 128:256] = jnp.where(lane8 < TS, r, l) * side


def comm_call(dest, roff, coff, wgt, tiles, rker, cker, f1, b1, f2, f3):
    vm = pl.BlockSpec(memory_space=pltpu.VMEM)
    sm = pl.BlockSpec(memory_space=pltpu.SMEM)
    return pl.pallas_call(
        comm_kernel,
        out_shape=[jax.ShapeDtypeStruct((152, 256), F32)] + W_SHAPES,
        in_specs=[sm] * 4 + [vm] * 7,
        out_specs=[vm] * 4,
        scratch_shapes=[
            pltpu.VMEM((3 * TS, TS), F32),
            pltpu.VMEM((TILES_DEV, 32, 128), F32),
            pltpu.VMEM((N_COL, 40, 128), F32),
            pltpu.VMEM((N_COL, 40, 128), F32),
            pltpu.VMEM((N_COL * TS, 256), BF),
            pltpu.VMEM((4, 8, 128), F32),
            pltpu.VMEM((8, 8, 128), F32),
            pltpu.SemaphoreType.DMA((N_COL,)),
            pltpu.SemaphoreType.DMA((N_COL,)),
            pltpu.SemaphoreType.DMA((8,)),
            pltpu.SemaphoreType.DMA((8,)),
        ],
        compiler_params=pltpu.CompilerParams(collective_id=0, has_side_effects=True, vmem_limit_bytes=32 << 20),
        name="coadd",
    )(dest, roff, coff, wgt, tiles, rker, cker, f1, b1, f2, f3)


def body(tiles, row_kernels, column_resample_kernels, destination, row_offset, col_offset, exposure_weight,
         first_filter, first_bias, second_filter, second_bias, third_filter, third_bias):
    taps = lambda f: jnp.transpose(f, (2, 3, 0, 1)).reshape(9, 32, 32)
    wide = lambda b: jnp.broadcast_to(b[:, None], (32, 256))
    p, w1, w2, w3 = comm_call(destination[:, 0], row_offset, col_offset, exposure_weight, tiles, row_kernels,
                              column_resample_kernels, first_filter.reshape(32, 9), first_bias[:, None],
                              taps(second_filter), taps(third_filter))
    out = conv_call(p, w1, w2, w3, wide(second_bias), wide(third_bias))
    return out.reshape(32, 128, 128)


def solution(mesh):
    held = P(("row", "col"))
    in_specs = (held,) * 7 + (P(),) * 6
    return jax.shard_map(body, mesh=mesh, in_specs=in_specs, out_specs=P(None, "row", "col"), check_vma=False)
```

```python
import functools
import jax
import jax.numpy as jnp
from jax import lax
from jax.experimental import pallas as pl
from jax.experimental.pallas import tpu as pltpu
from jax.sharding import PartitionSpec as P

BF = jnp.bfloat16
F32 = jnp.float32


def split(x):
    hi = x.astype(BF)
    return hi, (x - hi.astype(F32)).astype(BF)


def build_weights(f1_ref, vec_ref, f2_ref, f3_ref, w1_ref, w2_ref, w3_ref, bias_ref):
    for f_ref, w_ref in ((f2_ref, w2_ref), (f3_ref, w3_ref)):
        for dx in range(3):
            row = jnp.concatenate(
                [f_ref[dy * 3 + dx] for dy in range(3)] + [jnp.zeros((32, 160), F32)], axis=1)
            for yo in range(6):
                moved = row if yo == 0 else pltpu.roll(row, 32 * yo, 1)
                hi, lo = split(moved)
                w_ref[0, dx, yo * 32:(yo + 1) * 32, :] = hi
                w_ref[1, dx, yo * 32:(yo + 1) * 32, :] = lo
    rows = jnp.concatenate([f1_ref[k] for k in range(9)] + [vec_ref[k] for k in range(3)]
                           + [jnp.zeros((116, 32), F32)], axis=0)
    rows = jnp.concatenate([rows, jnp.zeros((128, 96), F32)], axis=1)
    turned = jnp.transpose(rows)[:32, :]
    hi, lo = split(turned)
    hi = hi.astype(F32)
    lo = lo.astype(F32)
    lane = lax.broadcasted_iota(jnp.int32, (32, 256), 1)
    base = jnp.where(lane == 144, hi[:, 9:10], 0.0) + jnp.where(lane == 145, lo[:, 9:10], 0.0)
    for yo in range(8):
        acc = base
        for part, w in enumerate((hi, hi, lo)):
            for dx in range(3):
                for dy in range(3):
                    k = dy * 3 + dx
                    acc = jnp.where(lane == part * 48 + dx * 16 + yo + dy, w[:, k:k + 1], acc)
        r = (yo % 2) * 128 + (yo // 2) * 32
        w1_ref[r:r + 32, :] = acc.astype(BF)
    for k in range(2):
        bias_ref[k] = jnp.broadcast_to(turned[:, 10 + k:11 + k], (32, 128))


def conv_body(row, col, p_ref, w1_ref, w2_ref, w3_ref, bias_ref, out_ref,
              ps, f_hi, f_lo, s_hi, s_lo):
    p = p_ref[...]
    ps[0] = pltpu.roll(p, 1, 1)
    ps[1] = p
    ps[2] = pltpu.roll(p, 255, 1)
    lane = lax.broadcasted_iota(jnp.int32, (1, 256), 1)
    dead = jnp.logical_or(jnp.logical_and(col == 0, lane >= 192),
                          jnp.logical_and(col == 15, jnp.logical_and(lane >= 128, lane < 192)))
    cmask = jnp.where(dead, 0.0, 1.0)
    sub = lax.broadcasted_iota(jnp.int32, (16, 256), 0)
    ones = jnp.where(sub < 2, 1.0, 0.0).astype(BF)
    pad = jnp.zeros((96, 256), BF)
    w1 = w1_ref[...]
    n_rows = 1024
    base = row * 128

    def valid(y):
        yy = base + y
        return jnp.where(jnp.logical_and(yy >= 0, yy < n_rows), 1.0, 0.0)

    @pl.loop(0, 18, unroll=3)
    def _(g):
        hs, ls = [], []
        for dx in range(3):
            h, l = split(ps[dx, pl.ds(pl.multiple_of(8 * g, 8), 16), :])
            hs.append(h)
            ls.append(l)
        rhs = jnp.concatenate(hs + ls + hs + [ones, pad], axis=0)
        acc = jnp.dot(w1, rhs, preferred_element_type=F32)
        for q in range(2):
            for m in range(4):
                mask = cmask * valid(8 * g + 2 * m + q - 6)
                v = jnp.maximum(acc[q * 128 + m * 32:q * 128 + m * 32 + 32, :], 0.0) * mask
                h, l = split(v)
                at = pl.ds(pl.multiple_of((4 * g + m) * 32, 32), 32)
                f_hi[q, at, :] = h
                f_lo[q, at, :] = l

    b2 = jnp.concatenate([bias_ref[0], bias_ref[0]], axis=1)

    @pl.loop(0, 24, unroll=4)
    def _(t):
        q = lax.rem(t, 2)
        m0 = jnp.minimum(6 * (t // 2), 62)
        at = pl.ds(pl.multiple_of(32 * m0, 64), 256)
        hi = f_hi[q, at, :]
        lo = f_lo[q, at, :]
        parts = []
        for dx in range(3):
            parts.append(jnp.dot(w2_ref[0, dx], hi, preferred_element_type=F32)
                         + jnp.dot(w2_ref[1, dx], hi, preferred_element_type=F32)
                         + jnp.dot(w2_ref[0, dx], lo, preferred_element_type=F32))
        acc = parts[1] + pltpu.roll(parts[0], 2, 1) + pltpu.roll(parts[2], 254, 1)
        n0 = m0 // 2
        for yo in range(6):
            mask = cmask * valid(2 * (m0 + yo) + q - 4)
            v = acc[yo * 32:yo * 32 + 32, :]
            v = jnp.maximum(v + b2, 0.0) * mask
            r = 2 * (yo % 2) + q
            at = pl.ds(pl.multiple_of((n0 + yo // 2) * 32, 32), 32)
            for k, sh in enumerate((pltpu.roll(v, 4, 1), v, pltpu.roll(v, 252, 1))):
                h, l = split(sh[:, :128])
                s_hi[k, r, at, :] = h
                s_lo[k, r, at, :] = l

    b3 = bias_ref[1]

    @pl.loop(0, 12, unroll=4)
    def _(t):
        half = lax.rem(t, 2)
        n0 = jnp.minimum(6 * (t // 2), 26)
        at = pl.ds(pl.multiple_of(32 * n0, 64), 256)
        hs, ls, wh, wl = [], [], [], []
        for dx in range(3):
            hs.append(jnp.concatenate([s_hi[dx, 2 * half, at, :], s_hi[dx, 2 * half + 1, at, :]], axis=1))
            ls.append(jnp.concatenate([s_lo[dx, 2 * half, at, :], s_lo[dx, 2 * half + 1, at, :]], axis=1))
            wh.append(w3_ref[0, dx])
            wl.append(w3_ref[1, dx])
        acc = jnp.dot(jnp.concatenate(wh + wl + wh, axis=1), jnp.concatenate(hs + hs + ls, axis=0),
                      preferred_element_type=F32)
        for e in range(2):
            for yo in range(6):
                v = acc[yo * 32:yo * 32 + 32, e * 128:e * 128 + 128] + b3
                y = 4 * (n0 + yo) + 2 * half + e
                for k in range(4):
                    out_ref[pl.ds(k * 1024 + y, 8, stride=128), :] = v[8 * k:8 * k + 8, :]


def conv_kernel(*refs):
    conv_body(lax.axis_index("row"), lax.axis_index("col"), *refs)


W_SHAPES = [jax.ShapeDtypeStruct((256, 256), BF), jax.ShapeDtypeStruct((2, 3, 192, 256), BF),
            jax.ShapeDtypeStruct((2, 3, 192, 256), BF), jax.ShapeDtypeStruct((2, 32, 128), F32)]


def conv_call(p, w1, w2, w3, bias):
    vm = pl.BlockSpec(memory_space=pltpu.VMEM)
    return pl.pallas_call(
        conv_kernel,
        out_shape=jax.ShapeDtypeStruct((4096, 128), F32),
        in_specs=[vm] * 5,
        out_specs=vm,
        scratch_shapes=[pltpu.VMEM((3, 152, 256), F32),
                        pltpu.VMEM((2, 74 * 32, 256), BF), pltpu.VMEM((2, 74 * 32, 256), BF),
                        pltpu.VMEM((3, 4, 34 * 32, 128), BF), pltpu.VMEM((3, 4, 34 * 32, 128), BF)],
        compiler_params=pltpu.CompilerParams(vmem_limit_bytes=48 << 20),
        name="convs",
    )(p, w1, w2, w3, bias)


N_ROW = 8
N_COL = 16
TILES_DEV = 8
TS = 64
MESH = pl.DeviceIdType.MESH


def dot3(ah, al, bh, bl, dims):
    d = functools.partial(lax.dot_general, dimension_numbers=(dims, ((), ())), preferred_element_type=F32)
    return d(ah, bh) + d(al, bh) + d(ah, bl)


def comm_kernel(dest_h, roff_h, coff_h, wgt_h, tiles_h, rker_h, cker_h, f1_h, b1_h, f2_h, b2_h, f3_h, b3_h,
                p_ref, w1_ref, w2_ref, w3_ref, bias_ref,
                dest, roff, coff, wgt, tiles, rker, ckpad, f1, vec, f2, f3, packed, send, recv, spread, pick,
                edge_out, edge_in, in_sem, send_sem, recv_sem, esend_sem, erecv_sem):
    fetches = [pltpu.make_async_copy(src, dst, in_sem.at[i]) for i, (src, dst) in enumerate((
        (rker_h, rker), (tiles_h, tiles), (cker_h, ckpad.at[:, pl.ds(TS, TS), :]), (coff_h, coff),
        (dest_h, dest), (roff_h, roff), (wgt_h, wgt), (f2_h, f2), (f3_h, f3),
        (f1_h, f1), (b1_h, vec.at[0]), (b2_h, vec.at[1]), (b3_h, vec.at[2])))]
    for f in fetches:
        f.start()
    row = lax.axis_index("row")
    col = lax.axis_index("col")
    up = lax.rem(row + N_ROW - 1, N_ROW)
    down = lax.rem(row + 1, N_ROW)
    left = lax.rem(col + N_COL - 1, N_COL)
    right = lax.rem(col + 1, N_COL)

    barrier = pltpu.get_barrier_semaphore()

    @pl.loop(1, N_COL)
    def _(k):
        pl.semaphore_signal(barrier, inc=1, device_id=(row, lax.rem(col + k, N_COL)), device_id_type=MESH)

    for r in (up, down):
        for c in (left, col, right):
            pl.semaphore_signal(barrier, inc=1, device_id=(r, c), device_id_type=MESH)

    blank = jnp.zeros((TILES_DEV, TS, TS), F32)
    ckpad[:, 0:TS, :] = blank
    ckpad[:, 2 * TS:3 * TS, :] = blank
    for f in fetches[:4]:
        f.wait()
    for t in range(TILES_DEV):
        rh, rl = split(rker[t])
        th, tl = split(tiles[t])
        mid = dot3(rh, rl, th, tl, ((1,), (0,)))
        placed = ckpad[t, pl.ds(TS - coff[0, t], 2 * TS), :]
        mh, ml = split(mid)
        ch, cl = split(placed)
        img = dot3(mh, ml, ch, cl, ((1,), (1,)))
        packed[t] = img[:32, :] + pltpu.roll(img[32:, :], 64, 1)
    for f in fetches[4:7]:
        f.wait()

    sub8 = lax.broadcasted_iota(jnp.int32, (8, 128), 0)

    @pl.loop(0, N_COL, unroll=4)
    def _(c):
        acc = None
        ro = jnp.float32(0.0)
        co = jnp.float32(0.0)
        w = jnp.float32(0.0)
        for t in range(TILES_DEV):
            hit = jnp.where(dest[0, t] == c, 1.0, 0.0)
            wt = hit * wgt[0, t]
            ro = ro + hit * roff[0, t].astype(F32)
            co = co + hit * coff[0, t].astype(F32)
            w = w + wt
            term = packed[t] * wt
            acc = term if acc is None else acc + term
        send[c, 0:32, :] = acc
        send[c, 32:40, :] = jnp.where(sub8 == 0, ro, jnp.where(sub8 == 1, co, w))

    pl.semaphore_wait(barrier, N_COL - 1 + 6)

    def tile_copy(k):
        c = lax.rem(col + k, N_COL)
        return pltpu.make_async_remote_copy(
            src_ref=send.at[c], dst_ref=recv.at[k], send_sem=send_sem.at[k], recv_sem=recv_sem.at[k],
            device_id=(row, c), device_id_type=MESH)

    @pl.loop(1, N_COL)
    def _(k):
        tile_copy(k).start()

    recv[0] = send[col]
    for f in fetches[7:]:
        f.wait()
    build_weights(f1, vec, f2, f3, w1_ref, w2_ref, w3_ref, bias_ref)

    lane = lax.broadcasted_iota(jnp.int32, (1, 128), 1).astype(F32)
    suby = lax.broadcasted_iota(jnp.int32, (128, 128), 0).astype(F32)
    lanes = lax.broadcasted_iota(jnp.int32, (128, 128), 1)
    lane_a = (lanes % TS).astype(F32)
    cover = jnp.zeros((128, 128), F32)
    for pair in range(N_COL // 2):
        ros = []
        for e in range(2):
            s = 2 * pair + e
            if s > 0:
                tile_copy(s).wait()
            pk = recv[s, 0:32, :]
            ro = recv[s, 32:33, :]
            co = recv[s, 33:34, :]
            w = recv[s, 34:35, :]
            at = lane - co
            inside = jnp.logical_and(at >= 0.0, at < float(TS))
            a = jnp.where(inside, pk, 0.0)
            b = jnp.where(inside, pltpu.roll(pk, 64, 1), 0.0)
            for half, v in enumerate((a, b)):
                h, l = split(v)
                r = s * TS + half * 32
                spread[r:r + 32, 0:128] = h
                spread[r:r + 32, 128:256] = l
            wcol = jnp.where(inside, w, 0.0)
            dy = suby - ro
            cover = cover + jnp.where(jnp.logical_and(dy >= 0.0, dy < float(TS)), wcol, 0.0)
            ros.append(ro)
        want = jnp.where(lanes < TS, ros[0], ros[1]) + lane_a
        pick[:, pair * 128:pair * 128 + 128] = jnp.where(suby == want, 1.0, 0.0).astype(BF)
    numer = jnp.dot(pick[...], spread[...], preferred_element_type=F32)
    coadd = (numer[:, :128] + numer[:, 128:]) / (1.0 + cover)

    edge_out[0] = coadd[0:8, :]
    edge_out[1] = coadd[120:128, :]
    lane8 = lax.broadcasted_iota(jnp.int32, (8, 128), 1)
    lcols = jnp.zeros((8, 128), F32)
    rcols = jnp.zeros((8, 128), F32)
    for k in range(16):
        blk = coadd[8 * k:8 * k + 8, :]
        here = jnp.logical_and(lane8 >= 8 * k, lane8 < 8 * k + 8)
        lcols = jnp.where(here, blk if k == 0 else pltpu.roll(blk, 8 * k, 1), lcols)
        rcols = jnp.where(here, blk if k == 15 else pltpu.roll(blk, 8 * k + 8, 1), rcols)
    edge_out[2] = lcols
    edge_out[3] = rcols
    plan = ((0, 1, (down, col)), (1, 0, (up, col)), (2, 3, (row, right)), (3, 2, (row, left)),
            (4, 1, (down, right)), (5, 1, (down, left)), (6, 0, (up, right)), (7, 0, (up, left)))
    copies = [pltpu.make_async_remote_copy(
        src_ref=edge_out.at[src], dst_ref=edge_in.at[slot], send_sem=esend_sem.at[slot],
        recv_sem=erecv_sem.at[slot], device_id=dev, device_id_type=MESH) for slot, src, dev in plan]
    for c in copies:
        c.start()
    p_ref[...] = jnp.zeros_like(p_ref)
    p_ref[7:135, 0:128] = coadd
    for c in copies:
        c.wait()

    has_up = jnp.where(row > 0, 1.0, 0.0)
    has_down = jnp.where(row < N_ROW - 1, 1.0, 0.0)
    has_left = jnp.where(col > 0, 1.0, 0.0)
    has_right = jnp.where(col < N_COL - 1, 1.0, 0.0)
    side = jnp.where(lane8 < TS, has_right, has_left)
    p_ref[0:7, 0:128] = edge_in[0][1:8, :] * has_up
    p_ref[135:142, 0:128] = edge_in[1][0:7, :] * has_down
    p_ref[0:7, 128:256] = (jnp.where(lane8 < TS, edge_in[5], edge_in[4]) * side * has_up)[1:8, :]
    p_ref[135:142, 128:256] = (jnp.where(lane8 < TS, edge_in[7], edge_in[6]) * side * has_down)[0:7, :]
    from_left = edge_in[2]
    from_right = edge_in[3]
    for k in range(16):
        r = from_right if k == 0 else pltpu.roll(from_right, 128 - 8 * k, 1)
        l = from_left if k == 15 else pltpu.roll(from_left, 120 - 8 * k, 1)
        p_ref[7 + 8 * k:15 + 8 * k, 128:256] = jnp.where(lane8 < TS, r, l) * side


def comm_call(*args):
    vm = pl.BlockSpec(memory_space=pltpu.VMEM)
    hbm = pl.BlockSpec(memory_space=pltpu.HBM)
    return pl.pallas_call(
        comm_kernel,
        out_shape=[jax.ShapeDtypeStruct((152, 256), F32)] + W_SHAPES,
        in_specs=[hbm] * 13,
        out_specs=[vm] * 5,
        scratch_shapes=[
            pltpu.SMEM((1, TILES_DEV), jnp.int32),
            pltpu.SMEM((1, TILES_DEV), jnp.int32),
            pltpu.SMEM((1, TILES_DEV), jnp.int32),
            pltpu.SMEM((1, TILES_DEV), F32),
            pltpu.VMEM((TILES_DEV, TS, TS), F32),
            pltpu.VMEM((TILES_DEV, TS, TS), F32),
            pltpu.VMEM((TILES_DEV, 3 * TS, TS), F32),
            pltpu.VMEM((9, 1, 32), F32),
            pltpu.VMEM((3, 1, 32), F32),
            pltpu.VMEM((9, 32, 32), F32),
            pltpu.VMEM((9, 32, 32), F32),
            pltpu.VMEM((TILES_DEV, 32, 128), F32),
            pltpu.VMEM((N_COL, 40, 128), F32),
            pltpu.VMEM((N_COL, 40, 128), F32),
            pltpu.VMEM((N_COL * TS, 256), BF),
            pltpu.VMEM((128, N_COL * TS), BF),
            pltpu.VMEM((4, 8, 128), F32),
            pltpu.VMEM((8, 8, 128), F32),
            pltpu.SemaphoreType.DMA((13,)),
            pltpu.SemaphoreType.DMA((N_COL,)),
            pltpu.SemaphoreType.DMA((N_COL,)),
            pltpu.SemaphoreType.DMA((8,)),
            pltpu.SemaphoreType.DMA((8,)),
        ],
        compiler_params=pltpu.CompilerParams(collective_id=0, has_side_effects=True, vmem_limit_bytes=32 << 20),
        name="coadd",
    )(*args)


def body(tiles, row_kernels, column_resample_kernels, destination, row_offset, col_offset, exposure_weight,
         first_filter, first_bias, second_filter, second_bias, third_filter, third_bias):
    line = lambda v: v.reshape(1, -1)
    taps = lambda f: jnp.transpose(f, (2, 3, 0, 1)).reshape(9, 32, 32)
    one = jnp.transpose(first_filter, (2, 3, 1, 0)).reshape(9, 1, 32)
    keep = lambda v: pltpu.with_memory_space_constraint(v, pltpu.HBM)
    p, w1, w2, w3, bias = comm_call(*map(keep, (
        destination.T, line(row_offset), line(col_offset), line(exposure_weight), tiles, row_kernels,
        column_resample_kernels, one, line(first_bias), taps(second_filter), line(second_bias),
        taps(third_filter), line(third_bias))))
    return conv_call(p, w1, w2, w3, bias).reshape(32, 128, 128)


def solution(mesh):
    held = P(("row", "col"))
    in_specs = (held,) * 7 + (P(),) * 6
    return jax.shard_map(body, mesh=mesh, in_specs=in_specs, out_specs=P(None, "row", "col"), check_vma=False)
```

```python
import functools
import jax
import jax.numpy as jnp
from jax import lax
from jax.experimental import pallas as pl
from jax.experimental.pallas import tpu as pltpu
from jax.sharding import PartitionSpec as P

BF = jnp.bfloat16
F32 = jnp.float32


def split(x):
    hi = x.astype(BF)
    return hi, (x - hi.astype(F32)).astype(BF)


def build_weights(f1_ref, vec_ref, f2_ref, f3_ref, w1_ref, w2_ref, w3_ref, bias_ref):
    for f_ref, w_ref in ((f2_ref, w2_ref), (f3_ref, w3_ref)):
        for dx in range(3):
            row = jnp.concatenate(
                [f_ref[dy * 3 + dx] for dy in range(3)] + [jnp.zeros((32, 160), F32)], axis=1)
            for yo in range(6):
                moved = row if yo == 0 else pltpu.roll(row, 32 * yo, 1)
                hi, lo = split(moved)
                w_ref[0, dx, yo * 32:(yo + 1) * 32, :] = hi
                w_ref[1, dx, yo * 32:(yo + 1) * 32, :] = lo
    rows = jnp.concatenate([f1_ref[k] for k in range(9)] + [vec_ref[k] for k in range(3)]
                           + [jnp.zeros((116, 32), F32)], axis=0)
    rows = jnp.concatenate([rows, jnp.zeros((128, 96), F32)], axis=1)
    turned = jnp.transpose(rows)[:32, :]
    hi, lo = split(turned)
    hi = hi.astype(F32)
    lo = lo.astype(F32)
    lane = lax.broadcasted_iota(jnp.int32, (32, 256), 1)
    base = jnp.where(lane == 144, hi[:, 9:10], 0.0) + jnp.where(lane == 145, lo[:, 9:10], 0.0)
    for yo in range(8):
        acc = base
        for part, w in enumerate((hi, hi, lo)):
            for dx in range(3):
                for dy in range(3):
                    k = dy * 3 + dx
                    acc = jnp.where(lane == part * 48 + dx * 16 + yo + dy, w[:, k:k + 1], acc)
        r = (yo % 2) * 128 + (yo // 2) * 32
        w1_ref[r:r + 32, :] = acc.astype(BF)
    for k in range(2):
        bias_ref[k] = jnp.broadcast_to(turned[:, 10 + k:11 + k], (32, 128))


def conv_body(row, col, p_ref, w1_ref, w2_ref, w3_ref, bias_ref, out_ref,
              ps, f_hi, f_lo, s_hi, s_lo, out_s, out_sem):
    p = p_ref[...]
    ps[0] = pltpu.roll(p, 1, 1)
    ps[1] = p
    ps[2] = pltpu.roll(p, 255, 1)
    lane = lax.broadcasted_iota(jnp.int32, (1, 256), 1)
    dead = jnp.logical_or(jnp.logical_and(col == 0, lane >= 192),
                          jnp.logical_and(col == 15, jnp.logical_and(lane >= 128, lane < 192)))
    cmask = jnp.where(dead, 0.0, 1.0)
    sub = lax.broadcasted_iota(jnp.int32, (16, 256), 0)
    ones = jnp.where(sub < 2, 1.0, 0.0).astype(BF)
    pad = jnp.zeros((96, 256), BF)
    w1 = w1_ref[...]
    n_rows = 1024
    base = row * 128

    def valid(y):
        yy = base + y
        return jnp.where(jnp.logical_and(yy >= 0, yy < n_rows), 1.0, 0.0)

    @pl.loop(0, 18, unroll=6)
    def _(g):
        hs, ls = [], []
        for dx in range(3):
            h, l = split(ps[dx, pl.ds(pl.multiple_of(8 * g, 8), 16), :])
            hs.append(h)
            ls.append(l)
        rhs = jnp.concatenate(hs + ls + hs + [ones, pad], axis=0)
        acc = jnp.dot(w1, rhs, preferred_element_type=F32)
        for q in range(2):
            for m in range(4):
                mask = cmask * valid(8 * g + 2 * m + q - 6)
                v = jnp.maximum(acc[q * 128 + m * 32:q * 128 + m * 32 + 32, :], 0.0) * mask
                h, l = split(v)
                at = pl.ds(pl.multiple_of((4 * g + m) * 32, 32), 32)
                f_hi[q, at, :] = h
                f_lo[q, at, :] = l

    b2 = jnp.concatenate([bias_ref[0], bias_ref[0]], axis=1)

    @pl.loop(0, 24, unroll=12)
    def _(t):
        q = lax.rem(t, 2)
        m0 = jnp.minimum(6 * (t // 2), 62)
        at = pl.ds(pl.multiple_of(32 * m0, 64), 256)
        hi = f_hi[q, at, :]
        lo = f_lo[q, at, :]
        parts = []
        for dx in range(3):
            parts.append(jnp.dot(w2_ref[0, dx], hi, preferred_element_type=F32)
                         + jnp.dot(w2_ref[1, dx], hi, preferred_element_type=F32)
                         + jnp.dot(w2_ref[0, dx], lo, preferred_element_type=F32))
        acc = parts[1] + pltpu.roll(parts[0], 2, 1) + pltpu.roll(parts[2], 254, 1)
        n0 = m0 // 2
        for yo in range(6):
            mask = cmask * valid(2 * (m0 + yo) + q - 4)
            v = acc[yo * 32:yo * 32 + 32, :]
            v = jnp.maximum(v + b2, 0.0) * mask
            r = 2 * (yo % 2) + q
            at = pl.ds(pl.multiple_of((n0 + yo // 2) * 32, 32), 32)
            for k, sh in enumerate((pltpu.roll(v, 4, 1), v, pltpu.roll(v, 252, 1))):
                h, l = split(sh[:, :128])
                s_hi[k, r, at, :] = h
                s_lo[k, r, at, :] = l

    b3 = bias_ref[1]

    whole = out_s.reshape(32, 128, 128)
    writes = []
    for step, (n0, first, count) in enumerate(
            ((0, 0, 24), (6, 24, 24), (12, 48, 24), (18, 72, 24), (24, 96, 8), (26, 104, 24))):
        at = pl.ds(32 * n0, 256)
        for half in range(2):
            hs, ls, wh, wl = [], [], [], []
            for dx in range(3):
                hs.append(jnp.concatenate([s_hi[dx, 2 * half, at, :], s_hi[dx, 2 * half + 1, at, :]], axis=1))
                ls.append(jnp.concatenate([s_lo[dx, 2 * half, at, :], s_lo[dx, 2 * half + 1, at, :]], axis=1))
                wh.append(w3_ref[0, dx])
                wl.append(w3_ref[1, dx])
            acc = jnp.dot(jnp.concatenate(wh + wl + wh, axis=1), jnp.concatenate(hs + hs + ls, axis=0),
                          preferred_element_type=F32)
            for e in range(2):
                for yo in range(6):
                    v = acc[yo * 32:yo * 32 + 32, e * 128:e * 128 + 128] + b3
                    y = 4 * (n0 + yo) + 2 * half + e
                    for k in range(4):
                        out_s[pl.ds(k * 1024 + y, 8, stride=128), :] = v[8 * k:8 * k + 8, :]
        rows = pl.ds(first, count)
        writes.append(pltpu.make_async_copy(whole.at[:, rows, :], out_ref.at[:, rows, :], out_sem.at[step]))
        writes[-1].start()
    for w in writes:
        w.wait()


def conv_kernel(*refs):
    conv_body(lax.axis_index("row"), lax.axis_index("col"), *refs)


W_SHAPES = [jax.ShapeDtypeStruct((256, 256), BF), jax.ShapeDtypeStruct((2, 3, 192, 256), BF),
            jax.ShapeDtypeStruct((2, 3, 192, 256), BF), jax.ShapeDtypeStruct((2, 32, 128), F32)]


def conv_call(p, w1, w2, w3, bias):
    vm = pl.BlockSpec(memory_space=pltpu.VMEM)
    return pl.pallas_call(
        conv_kernel,
        out_shape=jax.ShapeDtypeStruct((32, 128, 128), F32),
        in_specs=[vm] * 5,
        out_specs=pl.BlockSpec(memory_space=pltpu.HBM),
        scratch_shapes=[pltpu.VMEM((3, 152, 256), F32),
                        pltpu.VMEM((2, 74 * 32, 256), BF), pltpu.VMEM((2, 74 * 32, 256), BF),
                        pltpu.VMEM((3, 4, 34 * 32, 128), BF), pltpu.VMEM((3, 4, 34 * 32, 128), BF),
                        pltpu.VMEM((4096, 128), F32), pltpu.SemaphoreType.DMA((6,))],
        compiler_params=pltpu.CompilerParams(vmem_limit_bytes=48 << 20),
        name="convs",
    )(p, w1, w2, w3, bias)


N_ROW = 8
N_COL = 16
TILES_DEV = 8
TS = 64
MESH = pl.DeviceIdType.MESH
ORDER = (10, 1, 4, 3, 12, 2, 8, 5, 15, 7, 13, 6, 9, 14, 11)


def dot3(ah, al, bh, bl, dims):
    d = functools.partial(lax.dot_general, dimension_numbers=(dims, ((), ())), preferred_element_type=F32)
    return d(ah, bh) + d(al, bh) + d(ah, bl)


def comm_kernel(dest_h, roff_h, coff_h, wgt_h, tiles_h, rker_h, cker_h, f1_h, b1_h, f2_h, b2_h, f3_h, b3_h,
                p_ref, w1_ref, w2_ref, w3_ref, bias_ref,
                dest, roff, coff, wgt, tiles, rker, ckpad, f1, vec, f2, f3, packed, send, recv, spread, pick,
                edge_out, edge_in, in_sem, send_sem, recv_sem, esend_sem, erecv_sem):
    fetches = [pltpu.make_async_copy(src, dst, in_sem.at[i]) for i, (src, dst) in enumerate((
        (rker_h, rker), (tiles_h, tiles), (cker_h, ckpad.at[:, pl.ds(TS, TS), :]), (coff_h, coff),
        (dest_h, dest), (roff_h, roff), (wgt_h, wgt), (f2_h, f2), (f3_h, f3),
        (f1_h, f1), (b1_h, vec.at[0]), (b2_h, vec.at[1]), (b3_h, vec.at[2])))]
    for f in fetches:
        f.start()
    row = lax.axis_index("row")
    col = lax.axis_index("col")
    up = lax.rem(row + N_ROW - 1, N_ROW)
    down = lax.rem(row + 1, N_ROW)
    left = lax.rem(col + N_COL - 1, N_COL)
    right = lax.rem(col + 1, N_COL)

    barrier = pltpu.get_barrier_semaphore()

    @pl.loop(1, N_COL)
    def _(k):
        pl.semaphore_signal(barrier, inc=1, device_id=(row, lax.rem(col + k, N_COL)), device_id_type=MESH)

    for r in (up, down):
        for c in (left, col, right):
            pl.semaphore_signal(barrier, inc=1, device_id=(r, c), device_id_type=MESH)

    blank = jnp.zeros((TILES_DEV, TS, TS), F32)
    ckpad[:, 0:TS, :] = blank
    ckpad[:, 2 * TS:3 * TS, :] = blank
    for f in fetches[:4]:
        f.wait()
    for t in range(TILES_DEV):
        rh, rl = split(rker[t])
        th, tl = split(tiles[t])
        mid = dot3(rh, rl, th, tl, ((1,), (0,)))
        placed = ckpad[t, pl.ds(TS - coff[0, t], 2 * TS), :]
        mh, ml = split(mid)
        ch, cl = split(placed)
        img = dot3(mh, ml, ch, cl, ((1,), (1,)))
        packed[t] = img[:32, :] + pltpu.roll(img[32:, :], 64, 1)
    for f in fetches[4:7]:
        f.wait()

    sub8 = lax.broadcasted_iota(jnp.int32, (8, 128), 0)

    @pl.loop(0, N_COL, unroll=4)
    def _(c):
        acc = None
        ro = jnp.float32(0.0)
        co = jnp.float32(0.0)
        w = jnp.float32(0.0)
        for t in range(TILES_DEV):
            hit = jnp.where(dest[0, t] == c, 1.0, 0.0)
            wt = hit * wgt[0, t]
            ro = ro + hit * roff[0, t].astype(F32)
            co = co + hit * coff[0, t].astype(F32)
            w = w + wt
            term = packed[t] * wt
            acc = term if acc is None else acc + term
        send[c, 0:32, :] = acc
        send[c, 32:40, :] = jnp.where(sub8 == 0, ro, jnp.where(sub8 == 1, co, w))

    pl.semaphore_wait(barrier, N_COL - 1 + 6)

    def tile_copy(k):
        c = lax.rem(col + k, N_COL)
        return pltpu.make_async_remote_copy(
            src_ref=send.at[c], dst_ref=recv.at[k], send_sem=send_sem.at[k], recv_sem=recv_sem.at[k],
            device_id=(row, c), device_id_type=MESH)

    for k in ORDER:
        tile_copy(k).start()

    recv[0] = send[col]
    for f in fetches[7:]:
        f.wait()
    build_weights(f1, vec, f2, f3, w1_ref, w2_ref, w3_ref, bias_ref)

    lane = lax.broadcasted_iota(jnp.int32, (1, 128), 1).astype(F32)
    suby = lax.broadcasted_iota(jnp.int32, (128, 128), 0).astype(F32)
    lanes = lax.broadcasted_iota(jnp.int32, (128, 128), 1)
    lane_a = (lanes % TS).astype(F32)
    cover = jnp.zeros((128, 128), F32)
    for pair in range(N_COL // 2):
        ros = []
        for e in range(2):
            s = 2 * pair + e
            if s > 0:
                tile_copy(ORDER[s - 1]).wait()
            at = ORDER[s - 1] if s > 0 else 0
            pk = recv[at, 0:32, :]
            ro = recv[at, 32:33, :]
            co = recv[at, 33:34, :]
            w = recv[at, 34:35, :]
            off = lane - co
            inside = jnp.logical_and(off >= 0.0, off < float(TS))
            a = jnp.where(inside, pk, 0.0)
            b = jnp.where(inside, pltpu.roll(pk, 64, 1), 0.0)
            for half, v in enumerate((a, b)):
                h, l = split(v)
                r = s * TS + half * 32
                spread[r:r + 32, 0:128] = h
                spread[r:r + 32, 128:256] = l
            wcol = jnp.where(inside, w, 0.0)
            dy = suby - ro
            cover = cover + jnp.where(jnp.logical_and(dy >= 0.0, dy < float(TS)), wcol, 0.0)
            ros.append(ro)
        want = jnp.where(lanes < TS, ros[0], ros[1]) + lane_a
        pick[:, pair * 128:pair * 128 + 128] = jnp.where(suby == want, 1.0, 0.0).astype(BF)
    numer = jnp.dot(pick[...], spread[...], preferred_element_type=F32)
    coadd = (numer[:, :128] + numer[:, 128:]) / (1.0 + cover)

    edge_out[0] = coadd[0:8, :]
    edge_out[1] = coadd[120:128, :]
    lane8 = lax.broadcasted_iota(jnp.int32, (8, 128), 1)
    lcols = jnp.zeros((8, 128), F32)
    rcols = jnp.zeros((8, 128), F32)
    for k in range(16):
        blk = coadd[8 * k:8 * k + 8, :]
        here = jnp.logical_and(lane8 >= 8 * k, lane8 < 8 * k + 8)
        lcols = jnp.where(here, blk if k == 0 else pltpu.roll(blk, 8 * k, 1), lcols)
        rcols = jnp.where(here, blk if k == 15 else pltpu.roll(blk, 8 * k + 8, 1), rcols)
    edge_out[2] = lcols
    edge_out[3] = rcols
    plan = ((0, 1, (down, col)), (1, 0, (up, col)), (2, 3, (row, right)), (3, 2, (row, left)),
            (4, 1, (down, right)), (5, 1, (down, left)), (6, 0, (up, right)), (7, 0, (up, left)))
    copies = [pltpu.make_async_remote_copy(
        src_ref=edge_out.at[src], dst_ref=edge_in.at[slot], send_sem=esend_sem.at[slot],
        recv_sem=erecv_sem.at[slot], device_id=dev, device_id_type=MESH) for slot, src, dev in plan]
    for c in copies:
        c.start()
    p_ref[...] = jnp.zeros_like(p_ref)
    p_ref[7:135, 0:128] = coadd
    for c in copies:
        c.wait()

    has_up = jnp.where(row > 0, 1.0, 0.0)
    has_down = jnp.where(row < N_ROW - 1, 1.0, 0.0)
    has_left = jnp.where(col > 0, 1.0, 0.0)
    has_right = jnp.where(col < N_COL - 1, 1.0, 0.0)
    side = jnp.where(lane8 < TS, has_right, has_left)
    p_ref[0:7, 0:128] = edge_in[0][1:8, :] * has_up
    p_ref[135:142, 0:128] = edge_in[1][0:7, :] * has_down
    p_ref[0:7, 128:256] = (jnp.where(lane8 < TS, edge_in[5], edge_in[4]) * side * has_up)[1:8, :]
    p_ref[135:142, 128:256] = (jnp.where(lane8 < TS, edge_in[7], edge_in[6]) * side * has_down)[0:7, :]
    from_left = edge_in[2]
    from_right = edge_in[3]
    for k in range(16):
        r = from_right if k == 0 else pltpu.roll(from_right, 128 - 8 * k, 1)
        l = from_left if k == 15 else pltpu.roll(from_left, 120 - 8 * k, 1)
        p_ref[7 + 8 * k:15 + 8 * k, 128:256] = jnp.where(lane8 < TS, r, l) * side


def comm_call(*args):
    vm = pl.BlockSpec(memory_space=pltpu.VMEM)
    hbm = pl.BlockSpec(memory_space=pltpu.HBM)
    return pl.pallas_call(
        comm_kernel,
        out_shape=[jax.ShapeDtypeStruct((152, 256), F32)] + W_SHAPES,
        in_specs=[hbm] * 13,
        out_specs=[vm] * 5,
        scratch_shapes=[
            pltpu.SMEM((1, TILES_DEV), jnp.int32),
            pltpu.SMEM((1, TILES_DEV), jnp.int32),
            pltpu.SMEM((1, TILES_DEV), jnp.int32),
            pltpu.SMEM((1, TILES_DEV), F32),
            pltpu.VMEM((TILES_DEV, TS, TS), F32),
            pltpu.VMEM((TILES_DEV, TS, TS), F32),
            pltpu.VMEM((TILES_DEV, 3 * TS, TS), F32),
            pltpu.VMEM((9, 1, 32), F32),
            pltpu.VMEM((3, 1, 32), F32),
            pltpu.VMEM((9, 32, 32), F32),
            pltpu.VMEM((9, 32, 32), F32),
            pltpu.VMEM((TILES_DEV, 32, 128), F32),
            pltpu.VMEM((N_COL, 40, 128), F32),
            pltpu.VMEM((N_COL, 40, 128), F32),
            pltpu.VMEM((N_COL * TS, 256), BF),
            pltpu.VMEM((128, N_COL * TS), BF),
            pltpu.VMEM((4, 8, 128), F32),
            pltpu.VMEM((8, 8, 128), F32),
            pltpu.SemaphoreType.DMA((13,)),
            pltpu.SemaphoreType.DMA((N_COL,)),
            pltpu.SemaphoreType.DMA((N_COL,)),
            pltpu.SemaphoreType.DMA((8,)),
            pltpu.SemaphoreType.DMA((8,)),
        ],
        compiler_params=pltpu.CompilerParams(collective_id=0, has_side_effects=True, vmem_limit_bytes=32 << 20),
        name="coadd",
    )(*args)


def body(tiles, row_kernels, column_resample_kernels, destination, row_offset, col_offset, exposure_weight,
         first_filter, first_bias, second_filter, second_bias, third_filter, third_bias):
    line = lambda v: v.reshape(1, -1)
    taps = lambda f: jnp.transpose(f, (2, 3, 0, 1)).reshape(9, 32, 32)
    one = jnp.transpose(first_filter, (2, 3, 1, 0)).reshape(9, 1, 32)
    keep = lambda v: pltpu.with_memory_space_constraint(v, pltpu.HBM)
    p, w1, w2, w3, bias = comm_call(*map(keep, (
        destination.T, line(row_offset), line(col_offset), line(exposure_weight), tiles, row_kernels,
        column_resample_kernels, one, line(first_bias), taps(second_filter), line(second_bias),
        taps(third_filter), line(third_bias))))
    return conv_call(p, w1, w2, w3, bias)


def solution(mesh):
    held = P(("row", "col"))
    in_specs = (held,) * 7 + (P(),) * 6
    return jax.shard_map(body, mesh=mesh, in_specs=in_specs, out_specs=P(None, "row", "col"), check_vma=False)
```

```python
import functools
import jax
import jax.numpy as jnp
from jax import lax
from jax.experimental import pallas as pl
from jax.experimental.pallas import tpu as pltpu
from jax.sharding import PartitionSpec as P

BF = jnp.bfloat16
F32 = jnp.float32


def split(x):
    hi = x.astype(BF)
    return hi, (x - hi.astype(F32)).astype(BF)


def build_weights(f1_ref, vec_ref, f2_ref, f3_ref, w1_ref, w2_ref, w3_ref, bias_ref):
    for f_ref, w_ref in ((f2_ref, w2_ref), (f3_ref, w3_ref)):
        for dx in range(3):
            row = jnp.concatenate(
                [f_ref[dy * 3 + dx] for dy in range(3)] + [jnp.zeros((32, 160), F32)], axis=1)
            for yo in range(6):
                moved = row if yo == 0 else pltpu.roll(row, 32 * yo, 1)
                hi, lo = split(moved)
                w_ref[0, dx, yo * 32:(yo + 1) * 32, :] = hi
                w_ref[1, dx, yo * 32:(yo + 1) * 32, :] = lo
    rows = jnp.concatenate([f1_ref[k] for k in range(9)] + [vec_ref[k] for k in range(3)]
                           + [jnp.zeros((116, 32), F32)], axis=0)
    rows = jnp.concatenate([rows, jnp.zeros((128, 96), F32)], axis=1)
    turned = jnp.transpose(rows)[:32, :]
    hi, lo = split(turned)
    hi = hi.astype(F32)
    lo = lo.astype(F32)
    lane = lax.broadcasted_iota(jnp.int32, (32, 256), 1)
    base = jnp.where(lane == 144, hi[:, 9:10], 0.0) + jnp.where(lane == 145, lo[:, 9:10], 0.0)
    for yo in range(8):
        acc = base
        for part, w in enumerate((hi, hi, lo)):
            for dx in range(3):
                for dy in range(3):
                    k = dy * 3 + dx
                    acc = jnp.where(lane == part * 48 + dx * 16 + yo + dy, w[:, k:k + 1], acc)
        r = (yo % 2) * 128 + (yo // 2) * 32
        w1_ref[r:r + 32, :] = acc.astype(BF)
    for k in range(2):
        bias_ref[k] = jnp.broadcast_to(turned[:, 10 + k:11 + k], (32, 128))


def conv_body(row, col, p_ref, w1_ref, w2_ref, w3_ref, bias_ref, out_ref,
              ps, f_hi, f_lo, s_hi, s_lo, out_s, out_sem):
    p = p_ref[...]
    ps[0] = pltpu.roll(p, 1, 1)
    ps[1] = p
    ps[2] = pltpu.roll(p, 255, 1)
    lane = lax.broadcasted_iota(jnp.int32, (1, 256), 1)
    dead = jnp.logical_or(jnp.logical_and(col == 0, lane >= 192),
                          jnp.logical_and(col == 15, jnp.logical_and(lane >= 128, lane < 192)))
    cmask = jnp.where(dead, 0.0, 1.0)
    sub = lax.broadcasted_iota(jnp.int32, (16, 256), 0)
    ones = jnp.where(sub < 2, 1.0, 0.0).astype(BF)
    pad = jnp.zeros((96, 256), BF)
    w1 = w1_ref[...]
    n_rows = 1024
    base = row * 128

    def valid(y):
        yy = base + y
        return jnp.where(jnp.logical_and(yy >= 0, yy < n_rows), 1.0, 0.0)

    @pl.loop(0, 18, unroll=18)
    def _(g):
        hs, ls = [], []
        for dx in range(3):
            h, l = split(ps[dx, pl.ds(pl.multiple_of(8 * g, 8), 16), :])
            hs.append(h)
            ls.append(l)
        rhs = jnp.concatenate(hs + ls + hs + [ones, pad], axis=0)
        acc = jnp.dot(w1, rhs, preferred_element_type=F32)
        for q in range(2):
            for m in range(4):
                mask = cmask * valid(8 * g + 2 * m + q - 6)
                v = jnp.maximum(acc[q * 128 + m * 32:q * 128 + m * 32 + 32, :], 0.0) * mask
                h, l = split(v)
                at = pl.ds(pl.multiple_of((4 * g + m) * 32, 32), 32)
                f_hi[q, at, :] = h
                f_lo[q, at, :] = l

    b2 = jnp.concatenate([bias_ref[0], bias_ref[0]], axis=1)

    def second(hi, lo, places):
        parts = []
        for dx in range(3):
            parts.append(jnp.dot(w2_ref[0, dx], hi, preferred_element_type=F32)
                         + jnp.dot(w2_ref[1, dx], hi, preferred_element_type=F32)
                         + jnp.dot(w2_ref[0, dx], lo, preferred_element_type=F32))
        acc = parts[1] + pltpu.roll(parts[0], 2, 1) + pltpu.roll(parts[2], 254, 1)
        for yo, y, r, n in places:
            mask = cmask * valid(y)
            v = jnp.maximum(acc[yo * 32:yo * 32 + 32, :] + b2, 0.0) * mask
            at = pl.ds(pl.multiple_of(n * 32, 32), 32)
            for k, sh in enumerate((pltpu.roll(v, 4, 1), v, pltpu.roll(v, 252, 1))):
                h, l = split(sh[:, :128])
                s_hi[k, r, at, :] = h
                s_lo[k, r, at, :] = l

    @pl.loop(0, 22, unroll=22)
    def _(t):
        q = lax.rem(t, 2)
        m0 = 6 * (t // 2)
        at = pl.ds(pl.multiple_of(32 * m0, 64), 256)
        second(f_hi[q, at, :], f_lo[q, at, :],
               [(yo, 2 * (m0 + yo) + q - 4, 2 * (yo % 2) + q, m0 // 2 + yo // 2) for yo in range(6)])

    tail = pl.ds(66 * 32, 128)
    both = lambda f: jnp.concatenate([f[0, tail, :], f[1, tail, :]], axis=0)
    second(both(f_hi), both(f_lo),
           [(4 * q + e, 2 * (66 + e) + q - 4, 2 * e + q, 33) for q in range(2) for e in range(2)])

    b3 = bias_ref[1]

    whole = out_s.reshape(32, 128, 128)
    writes = []
    def third(pick_block, places):
        hs, ls, wh, wl = [], [], [], []
        for dx in range(3):
            hs.append(pick_block(s_hi, dx))
            ls.append(pick_block(s_lo, dx))
            wh.append(w3_ref[0, dx])
            wl.append(w3_ref[1, dx])
        acc = jnp.dot(jnp.concatenate(wh + wl + wh, axis=1), jnp.concatenate(hs + hs + ls, axis=0),
                      preferred_element_type=F32)
        for yo, e, y in places:
            v = acc[yo * 32:yo * 32 + 32, e * 128:e * 128 + 128] + b3
            for k in range(4):
                out_s[pl.ds(k * 1024 + y, 8, stride=128), :] = v[8 * k:8 * k + 8, :]

    for step in range(6):
        first, count = 24 * step, 24
        if step < 5:
            at = pl.ds(32 * 6 * step, 256)
            for half in range(2):
                third(lambda s, dx: jnp.concatenate([s[dx, 2 * half, at, :], s[dx, 2 * half + 1, at, :]], axis=1),
                      [(yo, e, 4 * (6 * step + yo) + 2 * half + e) for e in range(2) for yo in range(6)])
        else:
            count = 8
            at = pl.ds(32 * 30, 128)
            third(lambda s, dx: jnp.concatenate(
                [jnp.concatenate([s[dx, 2 * half, at, :], s[dx, 2 * half + 1, at, :]], axis=1) for half in range(2)],
                axis=0),
                [(4 * half + f, e, 4 * (30 + f) + 2 * half + e)
                 for half in range(2) for e in range(2) for f in range(2)])
        rows = pl.ds(first, count)
        writes.append(pltpu.make_async_copy(whole.at[:, rows, :], out_ref.at[:, rows, :], out_sem.at[step]))
        writes[-1].start()
    for w in writes:
        w.wait()


def conv_kernel(*refs):
    conv_body(lax.axis_index("row"), lax.axis_index("col"), *refs)


W_SHAPES = [jax.ShapeDtypeStruct((256, 256), BF), jax.ShapeDtypeStruct((2, 3, 192, 256), BF),
            jax.ShapeDtypeStruct((2, 3, 192, 256), BF), jax.ShapeDtypeStruct((2, 32, 128), F32)]


def conv_call(p, w1, w2, w3, bias):
    vm = pl.BlockSpec(memory_space=pltpu.VMEM)
    return pl.pallas_call(
        conv_kernel,
        out_shape=jax.ShapeDtypeStruct((32, 128, 128), F32),
        in_specs=[vm] * 5,
        out_specs=pl.BlockSpec(memory_space=pltpu.HBM),
        scratch_shapes=[pltpu.VMEM((3, 152, 256), F32),
                        pltpu.VMEM((2, 74 * 32, 256), BF), pltpu.VMEM((2, 74 * 32, 256), BF),
                        pltpu.VMEM((3, 4, 34 * 32, 128), BF), pltpu.VMEM((3, 4, 34 * 32, 128), BF),
                        pltpu.VMEM((4096, 128), F32), pltpu.SemaphoreType.DMA((6,))],
        compiler_params=pltpu.CompilerParams(vmem_limit_bytes=48 << 20),
        name="convs",
    )(p, w1, w2, w3, bias)


N_ROW = 8
N_COL = 16
TILES_DEV = 8
TS = 64
MESH = pl.DeviceIdType.MESH
ORDER = (10, 1, 4, 3, 12, 2, 8, 5, 15, 7, 13, 6, 9, 14, 11)


def dot3(ah, al, bh, bl, dims):
    d = functools.partial(lax.dot_general, dimension_numbers=(dims, ((), ())), preferred_element_type=F32)
    return d(ah, bh) + d(al, bh) + d(ah, bl)


def comm_kernel(dest_h, roff_h, coff_h, wgt_h, tiles_h, rker_h, cker_h, f1_h, b1_h, f2_h, b2_h, f3_h, b3_h,
                p_ref, w1_ref, w2_ref, w3_ref, bias_ref,
                dest, roff, coff, wgt, tiles, rker, ckpad, f1, vec, f2, f3, packed, send, recv, spread, pick,
                edge_out, edge_in, in_sem, send_sem, recv_sem, esend_sem, erecv_sem):
    fetches = [pltpu.make_async_copy(src, dst, in_sem.at[i]) for i, (src, dst) in enumerate((
        (rker_h, rker), (tiles_h, tiles), (cker_h, ckpad.at[:, pl.ds(TS, TS), :]), (coff_h, coff),
        (dest_h, dest), (roff_h, roff), (wgt_h, wgt), (f2_h, f2), (f3_h, f3),
        (f1_h, f1), (b1_h, vec.at[0]), (b2_h, vec.at[1]), (b3_h, vec.at[2])))]
    for f in fetches:
        f.start()
    row = lax.axis_index("row")
    col = lax.axis_index("col")
    up = lax.rem(row + N_ROW - 1, N_ROW)
    down = lax.rem(row + 1, N_ROW)
    left = lax.rem(col + N_COL - 1, N_COL)
    right = lax.rem(col + 1, N_COL)

    barrier = pltpu.get_barrier_semaphore()

    @pl.loop(1, N_COL)
    def _(k):
        pl.semaphore_signal(barrier, inc=1, device_id=(row, lax.rem(col + k, N_COL)), device_id_type=MESH)

    for r in (up, down):
        for c in (left, col, right):
            pl.semaphore_signal(barrier, inc=1, device_id=(r, c), device_id_type=MESH)

    blank = jnp.zeros((TILES_DEV, TS, TS), F32)
    ckpad[:, 0:TS, :] = blank
    ckpad[:, 2 * TS:3 * TS, :] = blank
    for f in fetches[:4]:
        f.wait()
    for t in range(TILES_DEV):
        rh, rl = split(rker[t])
        th, tl = split(tiles[t])
        mid = dot3(rh, rl, th, tl, ((1,), (0,)))
        placed = ckpad[t, pl.ds(TS - coff[0, t], 2 * TS), :]
        mh, ml = split(mid)
        ch, cl = split(placed)
        img = dot3(mh, ml, ch, cl, ((1,), (1,)))
        packed[t] = img[:32, :] + pltpu.roll(img[32:, :], 64, 1)
    for f in fetches[4:7]:
        f.wait()

    sub8 = lax.broadcasted_iota(jnp.int32, (8, 128), 0)

    @pl.loop(0, N_COL, unroll=4)
    def _(c):
        acc = None
        ro = jnp.float32(0.0)
        co = jnp.float32(0.0)
        w = jnp.float32(0.0)
        for t in range(TILES_DEV):
            hit = jnp.where(dest[0, t] == c, 1.0, 0.0)
            wt = hit * wgt[0, t]
            ro = ro + hit * roff[0, t].astype(F32)
            co = co + hit * coff[0, t].astype(F32)
            w = w + wt
            term = packed[t] * wt
            acc = term if acc is None else acc + term
        send[c, 0:32, :] = acc
        send[c, 32:40, :] = jnp.where(sub8 == 0, ro, jnp.where(sub8 == 1, co, w))

    pl.semaphore_wait(barrier, N_COL - 1 + 6)

    def tile_copy(k):
        c = lax.rem(col + k, N_COL)
        return pltpu.make_async_remote_copy(
            src_ref=send.at[c], dst_ref=recv.at[k], send_sem=send_sem.at[k], recv_sem=recv_sem.at[k],
            device_id=(row, c), device_id_type=MESH)

    for k in ORDER:
        tile_copy(k).start()

    recv[0] = send[col]
    for f in fetches[7:]:
        f.wait()
    build_weights(f1, vec, f2, f3, w1_ref, w2_ref, w3_ref, bias_ref)

    lane = lax.broadcasted_iota(jnp.int32, (1, 128), 1).astype(F32)
    suby = lax.broadcasted_iota(jnp.int32, (128, 128), 0).astype(F32)
    lanes = lax.broadcasted_iota(jnp.int32, (128, 128), 1)
    lane_a = (lanes % TS).astype(F32)
    cover = jnp.zeros((128, 128), F32)
    for pair in range(N_COL // 2):
        ros = []
        for e in range(2):
            s = 2 * pair + e
            if s > 0:
                tile_copy(ORDER[s - 1]).wait()
            at = ORDER[s - 1] if s > 0 else 0
            pk = recv[at, 0:32, :]
            ro = recv[at, 32:33, :]
            co = recv[at, 33:34, :]
            w = recv[at, 34:35, :]
            off = lane - co
            inside = jnp.logical_and(off >= 0.0, off < float(TS))
            a = jnp.where(inside, pk, 0.0)
            b = jnp.where(inside, pltpu.roll(pk, 64, 1), 0.0)
            for half, v in enumerate((a, b)):
                h, l = split(v)
                r = s * TS + half * 32
                spread[r:r + 32, 0:128] = h
                spread[r:r + 32, 128:256] = l
            wcol = jnp.where(inside, w, 0.0)
            dy = suby - ro
            cover = cover + jnp.where(jnp.logical_and(dy >= 0.0, dy < float(TS)), wcol, 0.0)
            ros.append(ro)
        want = jnp.where(lanes < TS, ros[0], ros[1]) + lane_a
        pick[:, pair * 128:pair * 128 + 128] = jnp.where(suby == want, 1.0, 0.0).astype(BF)
    numer = jnp.dot(pick[...], spread[...], preferred_element_type=F32)
    coadd = (numer[:, :128] + numer[:, 128:]) / (1.0 + cover)

    edge_out[0] = coadd[0:8, :]
    edge_out[1] = coadd[120:128, :]
    lane8 = lax.broadcasted_iota(jnp.int32, (8, 128), 1)
    lcols = jnp.zeros((8, 128), F32)
    rcols = jnp.zeros((8, 128), F32)
    for k in range(16):
        blk = coadd[8 * k:8 * k + 8, :]
        here = jnp.logical_and(lane8 >= 8 * k, lane8 < 8 * k + 8)
        lcols = jnp.where(here, blk if k == 0 else pltpu.roll(blk, 8 * k, 1), lcols)
        rcols = jnp.where(here, blk if k == 15 else pltpu.roll(blk, 8 * k + 8, 1), rcols)
    edge_out[2] = lcols
    edge_out[3] = rcols
    plan = ((0, 1, (down, col)), (1, 0, (up, col)), (2, 3, (row, right)), (3, 2, (row, left)),
            (4, 1, (down, right)), (5, 1, (down, left)), (6, 0, (up, right)), (7, 0, (up, left)))
    copies = [pltpu.make_async_remote_copy(
        src_ref=edge_out.at[src], dst_ref=edge_in.at[slot], send_sem=esend_sem.at[slot],
        recv_sem=erecv_sem.at[slot], device_id=dev, device_id_type=MESH) for slot, src, dev in plan]
    for c in copies:
        c.start()
    p_ref[...] = jnp.zeros_like(p_ref)
    p_ref[7:135, 0:128] = coadd
    for c in copies:
        c.wait()

    has_up = jnp.where(row > 0, 1.0, 0.0)
    has_down = jnp.where(row < N_ROW - 1, 1.0, 0.0)
    has_left = jnp.where(col > 0, 1.0, 0.0)
    has_right = jnp.where(col < N_COL - 1, 1.0, 0.0)
    side = jnp.where(lane8 < TS, has_right, has_left)
    p_ref[0:7, 0:128] = edge_in[0][1:8, :] * has_up
    p_ref[135:142, 0:128] = edge_in[1][0:7, :] * has_down
    p_ref[0:7, 128:256] = (jnp.where(lane8 < TS, edge_in[5], edge_in[4]) * side * has_up)[1:8, :]
    p_ref[135:142, 128:256] = (jnp.where(lane8 < TS, edge_in[7], edge_in[6]) * side * has_down)[0:7, :]
    from_left = edge_in[2]
    from_right = edge_in[3]
    for k in range(16):
        r = from_right if k == 0 else pltpu.roll(from_right, 128 - 8 * k, 1)
        l = from_left if k == 15 else pltpu.roll(from_left, 120 - 8 * k, 1)
        p_ref[7 + 8 * k:15 + 8 * k, 128:256] = jnp.where(lane8 < TS, r, l) * side


def comm_call(*args):
    vm = pl.BlockSpec(memory_space=pltpu.VMEM)
    hbm = pl.BlockSpec(memory_space=pltpu.HBM)
    return pl.pallas_call(
        comm_kernel,
        out_shape=[jax.ShapeDtypeStruct((152, 256), F32)] + W_SHAPES,
        in_specs=[hbm] * 13,
        out_specs=[vm] * 5,
        scratch_shapes=[
            pltpu.SMEM((1, TILES_DEV), jnp.int32),
            pltpu.SMEM((1, TILES_DEV), jnp.int32),
            pltpu.SMEM((1, TILES_DEV), jnp.int32),
            pltpu.SMEM((1, TILES_DEV), F32),
            pltpu.VMEM((TILES_DEV, TS, TS), F32),
            pltpu.VMEM((TILES_DEV, TS, TS), F32),
            pltpu.VMEM((TILES_DEV, 3 * TS, TS), F32),
            pltpu.VMEM((9, 1, 32), F32),
            pltpu.VMEM((3, 1, 32), F32),
            pltpu.VMEM((9, 32, 32), F32),
            pltpu.VMEM((9, 32, 32), F32),
            pltpu.VMEM((TILES_DEV, 32, 128), F32),
            pltpu.VMEM((N_COL, 40, 128), F32),
            pltpu.VMEM((N_COL, 40, 128), F32),
            pltpu.VMEM((N_COL * TS, 256), BF),
            pltpu.VMEM((128, N_COL * TS), BF),
            pltpu.VMEM((4, 8, 128), F32),
            pltpu.VMEM((8, 8, 128), F32),
            pltpu.SemaphoreType.DMA((13,)),
            pltpu.SemaphoreType.DMA((N_COL,)),
            pltpu.SemaphoreType.DMA((N_COL,)),
            pltpu.SemaphoreType.DMA((8,)),
            pltpu.SemaphoreType.DMA((8,)),
        ],
        compiler_params=pltpu.CompilerParams(collective_id=0, has_side_effects=True, vmem_limit_bytes=32 << 20),
        name="coadd",
    )(*args)


def body(tiles, row_kernels, column_resample_kernels, destination, row_offset, col_offset, exposure_weight,
         first_filter, first_bias, second_filter, second_bias, third_filter, third_bias):
    line = lambda v: v.reshape(1, -1)
    taps = lambda f: jnp.transpose(f, (2, 3, 0, 1)).reshape(9, 32, 32)
    one = jnp.transpose(first_filter, (2, 3, 1, 0)).reshape(9, 1, 32)
    keep = lambda v: pltpu.with_memory_space_constraint(v, pltpu.HBM)
    p, w1, w2, w3, bias = comm_call(*map(keep, (
        destination.T, line(row_offset), line(col_offset), line(exposure_weight), tiles, row_kernels,
        column_resample_kernels, one, line(first_bias), taps(second_filter), line(second_bias),
        taps(third_filter), line(third_bias))))
    return conv_call(p, w1, w2, w3, bias)


def solution(mesh):
    held = P(("row", "col"))
    in_specs = (held,) * 7 + (P(),) * 6
    return jax.shard_map(body, mesh=mesh, in_specs=in_specs, out_specs=P(None, "row", "col"), check_vma=False)
```

```python
import functools
import jax
import jax.numpy as jnp
from jax import lax
from jax.experimental import pallas as pl
from jax.experimental.pallas import tpu as pltpu
from jax.sharding import PartitionSpec as P

BF = jnp.bfloat16
F32 = jnp.float32


def split(x):
    hi = x.astype(BF)
    return hi, (x - hi.astype(F32)).astype(BF)


def build_weights(f1_ref, vec_ref, f2_ref, f3_ref, w1_ref, w2_ref, w3_ref, bias_ref):
    for f_ref, w_ref in ((f2_ref, w2_ref), (f3_ref, w3_ref)):
        for dx in range(3):
            row = jnp.concatenate(
                [f_ref[dy * 3 + dx] for dy in range(3)] + [jnp.zeros((32, 160), F32)], axis=1)
            for yo in range(6):
                moved = row if yo == 0 else pltpu.roll(row, 32 * yo, 1)
                hi, lo = split(moved)
                w_ref[0, dx, yo * 32:(yo + 1) * 32, :] = hi
                w_ref[1, dx, yo * 32:(yo + 1) * 32, :] = lo
    rows = jnp.concatenate([f1_ref[k] for k in range(9)] + [vec_ref[k] for k in range(3)]
                           + [jnp.zeros((116, 32), F32)], axis=0)
    rows = jnp.concatenate([rows, jnp.zeros((128, 96), F32)], axis=1)
    turned = jnp.transpose(rows)[:32, :]
    hi, lo = split(turned)
    hi = hi.astype(F32)
    lo = lo.astype(F32)
    lane = lax.broadcasted_iota(jnp.int32, (32, 256), 1)
    base = jnp.where(lane == 144, hi[:, 9:10], 0.0) + jnp.where(lane == 145, lo[:, 9:10], 0.0)
    for yo in range(8):
        acc = base
        for part, w in enumerate((hi, hi, lo)):
            for dx in range(3):
                for dy in range(3):
                    k = dy * 3 + dx
                    acc = jnp.where(lane == part * 48 + dx * 16 + yo + dy, w[:, k:k + 1], acc)
        r = (yo % 2) * 128 + (yo // 2) * 32
        w1_ref[r:r + 32, :] = acc.astype(BF)
    for k in range(2):
        bias_ref[k] = jnp.broadcast_to(turned[:, 10 + k:11 + k], (32, 128))


def conv_body(row, col, p_ref, w1_ref, w2_ref, w3_ref, bias_ref, out_ref,
              ps, f_hi, f_lo, s_hi, s_lo, out_s, out_sem):
    p = p_ref[...]
    ps[0] = pltpu.roll(p, 1, 1)
    ps[1] = p
    ps[2] = pltpu.roll(p, 255, 1)
    lane = lax.broadcasted_iota(jnp.int32, (1, 256), 1)
    dead = jnp.logical_or(jnp.logical_and(col == 0, lane >= 192),
                          jnp.logical_and(col == 15, jnp.logical_and(lane >= 128, lane < 192)))
    cmask = jnp.where(dead, 0.0, 1.0)
    sub = lax.broadcasted_iota(jnp.int32, (16, 256), 0)
    ones = jnp.where(sub < 2, 1.0, 0.0).astype(BF)
    pad = jnp.zeros((96, 256), BF)
    w1 = w1_ref[...]
    n_rows = 1024
    base = row * 128

    def valid(y):
        yy = base + y
        return jnp.where(jnp.logical_and(yy >= 0, yy < n_rows), 1.0, 0.0)

    @pl.loop(0, 18, unroll=18)
    def _(g):
        hs, ls = [], []
        for dx in range(3):
            h, l = split(ps[dx, pl.ds(pl.multiple_of(8 * g, 8), 16), :])
            hs.append(h)
            ls.append(l)
        rhs = jnp.concatenate(hs + ls + hs + [ones, pad], axis=0)
        acc = jnp.dot(w1, rhs, preferred_element_type=F32)
        for q in range(2):
            for m in range(4):
                mask = cmask * valid(8 * g + 2 * m + q - 6)
                v = jnp.maximum(acc[q * 128 + m * 32:q * 128 + m * 32 + 32, :], 0.0) * mask
                h, l = split(v)
                at = pl.ds(pl.multiple_of((4 * g + m) * 32, 32), 32)
                f_hi[q, at, :] = h
                f_lo[q, at, :] = l

    b2 = jnp.concatenate([bias_ref[0], bias_ref[0]], axis=1)

    def second(hi, lo, places):
        parts = []
        for dx in range(3):
            parts.append(jnp.dot(w2_ref[0, dx], hi, preferred_element_type=F32)
                         + jnp.dot(w2_ref[1, dx], hi, preferred_element_type=F32)
                         + jnp.dot(w2_ref[0, dx], lo, preferred_element_type=F32))
        acc = parts[1] + pltpu.roll(parts[0], 2, 1) + pltpu.roll(parts[2], 254, 1)
        for yo, y, r, n in places:
            mask = cmask * valid(y)
            v = jnp.maximum(acc[yo * 32:yo * 32 + 32, :] + b2, 0.0) * mask
            at = pl.ds(pl.multiple_of(n * 32, 32), 32)
            for k, sh in enumerate((pltpu.roll(v, 4, 1), v, pltpu.roll(v, 252, 1))):
                h, l = split(sh[:, :128])
                s_hi[k, r, at, :] = h
                s_lo[k, r, at, :] = l

    @pl.loop(0, 22, unroll=22)
    def _(t):
        q = lax.rem(t, 2)
        m0 = 6 * (t // 2)
        at = pl.ds(pl.multiple_of(32 * m0, 64), 256)
        second(f_hi[q, at, :], f_lo[q, at, :],
               [(yo, 2 * (m0 + yo) + q - 4, 2 * (yo % 2) + q, m0 // 2 + yo // 2) for yo in range(6)])

    tail = pl.ds(66 * 32, 128)
    both = lambda f: jnp.concatenate([f[0, tail, :], f[1, tail, :]], axis=0)
    second(both(f_hi), both(f_lo),
           [(4 * q + e, 2 * (66 + e) + q - 4, 2 * e + q, 33) for q in range(2) for e in range(2)])

    b3 = bias_ref[1]

    whole = out_s.reshape(32, 128, 128)
    writes = []
    def third(pick_block, places):
        hs, ls, wh, wl = [], [], [], []
        for dx in range(3):
            hs.append(pick_block(s_hi, dx))
            ls.append(pick_block(s_lo, dx))
            wh.append(w3_ref[0, dx])
            wl.append(w3_ref[1, dx])
        acc = jnp.dot(jnp.concatenate(wh + wl + wh, axis=1), jnp.concatenate(hs + hs + ls, axis=0),
                      preferred_element_type=F32)
        for yo, e, y in places:
            v = acc[yo * 32:yo * 32 + 32, e * 128:e * 128 + 128] + b3
            for k in range(4):
                out_s[pl.ds(k * 1024 + y, 8, stride=128), :] = v[8 * k:8 * k + 8, :]

    for step in range(6):
        first, count = 24 * step, 24
        if step < 5:
            at = pl.ds(32 * 6 * step, 256)
            for half in range(2):
                third(lambda s, dx: jnp.concatenate([s[dx, 2 * half, at, :], s[dx, 2 * half + 1, at, :]], axis=1),
                      [(yo, e, 4 * (6 * step + yo) + 2 * half + e) for e in range(2) for yo in range(6)])
        else:
            count = 8
            at = pl.ds(32 * 30, 128)
            third(lambda s, dx: jnp.concatenate(
                [jnp.concatenate([s[dx, 2 * half, at, :], s[dx, 2 * half + 1, at, :]], axis=1) for half in range(2)],
                axis=0),
                [(4 * half + f, e, 4 * (30 + f) + 2 * half + e)
                 for half in range(2) for e in range(2) for f in range(2)])
        rows = pl.ds(first, count)
        writes.append(pltpu.make_async_copy(whole.at[:, rows, :], out_ref.at[:, rows, :], out_sem.at[step]))
        writes[-1].start()
    for w in writes:
        w.wait()


def conv_kernel(*refs):
    conv_body(lax.axis_index("row"), lax.axis_index("col"), *refs)


W_SHAPES = [jax.ShapeDtypeStruct((256, 256), BF), jax.ShapeDtypeStruct((2, 3, 192, 256), BF),
            jax.ShapeDtypeStruct((2, 3, 192, 256), BF), jax.ShapeDtypeStruct((2, 32, 128), F32)]


def conv_call(p, w1, w2, w3, bias):
    vm = pl.BlockSpec(memory_space=pltpu.VMEM)
    return pl.pallas_call(
        conv_kernel,
        out_shape=jax.ShapeDtypeStruct((32, 128, 128), F32),
        in_specs=[vm] * 5,
        out_specs=pl.BlockSpec(memory_space=pltpu.HBM),
        scratch_shapes=[pltpu.VMEM((3, 152, 256), F32),
                        pltpu.VMEM((2, 74 * 32, 256), BF), pltpu.VMEM((2, 74 * 32, 256), BF),
                        pltpu.VMEM((3, 4, 34 * 32, 128), BF), pltpu.VMEM((3, 4, 34 * 32, 128), BF),
                        pltpu.VMEM((4096, 128), F32), pltpu.SemaphoreType.DMA((6,))],
        compiler_params=pltpu.CompilerParams(vmem_limit_bytes=48 << 20),
        name="convs",
    )(p, w1, w2, w3, bias)


N_ROW = 8
N_COL = 16
TILES_DEV = 8
TS = 64
MESH = pl.DeviceIdType.MESH
ORDER = (10, 1, 4, 3, 12, 2, 8, 5, 15, 7, 13, 6, 9, 14, 11)


def dot3(ah, al, bh, bl, dims):
    d = functools.partial(lax.dot_general, dimension_numbers=(dims, ((), ())), preferred_element_type=F32)
    return d(ah, bh) + d(al, bh) + d(ah, bl)


def comm_kernel(dest_h, roff_h, coff_h, wgt_h, tiles_h, rker_h, cker_h, f1_h, b1_h, f2_h, b2_h, f3_h, b3_h,
                p_ref, w1_ref, w2_ref, w3_ref, bias_ref,
                dest, roff, coff, wgt, tiles, rker, ckpad, f1, vec, f2, f3, packed, send, recv, spread, pick,
                edge_out, edge_in, in_sem, send_sem, recv_sem, esend_sem, erecv_sem):
    fetches = [pltpu.make_async_copy(src, dst, in_sem.at[i]) for i, (src, dst) in enumerate((
        (rker_h, rker), (tiles_h, tiles), (cker_h, ckpad.at[:, pl.ds(TS, TS), :]), (coff_h, coff),
        (dest_h, dest), (roff_h, roff), (wgt_h, wgt), (f2_h, f2), (f3_h, f3),
        (f1_h, f1), (b1_h, vec.at[0]), (b2_h, vec.at[1]), (b3_h, vec.at[2])))]
    for f in fetches:
        f.start()
    row = lax.axis_index("row")
    col = lax.axis_index("col")
    up = lax.rem(row + N_ROW - 1, N_ROW)
    down = lax.rem(row + 1, N_ROW)
    left = lax.rem(col + N_COL - 1, N_COL)
    right = lax.rem(col + 1, N_COL)

    barrier = pltpu.get_barrier_semaphore()

    @pl.loop(1, N_COL)
    def _(k):
        pl.semaphore_signal(barrier, inc=1, device_id=(row, lax.rem(col + k, N_COL)), device_id_type=MESH)

    for r in (up, down):
        for c in (left, col, right):
            pl.semaphore_signal(barrier, inc=1, device_id=(r, c), device_id_type=MESH)

    blank = jnp.zeros((TILES_DEV, TS, TS), F32)
    ckpad[:, 0:TS, :] = blank
    ckpad[:, 2 * TS:3 * TS, :] = blank
    for f in fetches[:4]:
        f.wait()
    for t in range(TILES_DEV):
        rh, rl = split(rker[t])
        th, tl = split(tiles[t])
        mid = dot3(rh, rl, th, tl, ((1,), (0,)))
        placed = ckpad[t, pl.ds(TS - coff[0, t], 2 * TS), :]
        mh, ml = split(mid)
        ch, cl = split(placed)
        img = dot3(mh, ml, ch, cl, ((1,), (1,)))
        packed[t] = img[:32, :] + pltpu.roll(img[32:, :], 64, 1)
    for f in fetches[4:7]:
        f.wait()

    sub8 = lax.broadcasted_iota(jnp.int32, (8, 128), 0)

    def fill(c, slot):
        acc = None
        ro = jnp.float32(0.0)
        co = jnp.float32(0.0)
        w = jnp.float32(0.0)
        for t in range(TILES_DEV):
            hit = jnp.where(dest[0, t] == c, 1.0, 0.0)
            wt = hit * wgt[0, t]
            ro = ro + hit * roff[0, t].astype(F32)
            co = co + hit * coff[0, t].astype(F32)
            w = w + wt
            term = packed[t] * wt
            acc = term if acc is None else acc + term
        slot[0:32, :] = acc
        slot[32:40, :] = jnp.where(sub8 == 0, ro, jnp.where(sub8 == 1, co, w))

    pl.semaphore_wait(barrier, N_COL - 1 + 6)

    def tile_copy(k):
        c = lax.rem(col + k, N_COL)
        return pltpu.make_async_remote_copy(
            src_ref=send.at[c], dst_ref=recv.at[k], send_sem=send_sem.at[k], recv_sem=recv_sem.at[k],
            device_id=(row, c), device_id_type=MESH)

    for k in ORDER:
        c = lax.rem(col + k, N_COL)
        fill(c, send.at[c])
        tile_copy(k).start()

    fill(col, recv.at[0])
    for f in fetches[7:]:
        f.wait()
    build_weights(f1, vec, f2, f3, w1_ref, w2_ref, w3_ref, bias_ref)

    lane = lax.broadcasted_iota(jnp.int32, (1, 128), 1).astype(F32)
    suby = lax.broadcasted_iota(jnp.int32, (128, 128), 0).astype(F32)
    lanes = lax.broadcasted_iota(jnp.int32, (128, 128), 1)
    lane_a = (lanes % TS).astype(F32)
    cover = jnp.zeros((128, 128), F32)
    for pair in range(N_COL // 2):
        ros = []
        for e in range(2):
            s = 2 * pair + e
            if s > 0:
                tile_copy(ORDER[s - 1]).wait()
            at = ORDER[s - 1] if s > 0 else 0
            pk = recv[at, 0:32, :]
            ro = recv[at, 32:33, :]
            co = recv[at, 33:34, :]
            w = recv[at, 34:35, :]
            off = lane - co
            inside = jnp.logical_and(off >= 0.0, off < float(TS))
            a = jnp.where(inside, pk, 0.0)
            b = jnp.where(inside, pltpu.roll(pk, 64, 1), 0.0)
            for half, v in enumerate((a, b)):
                h, l = split(v)
                r = s * TS + half * 32
                spread[r:r + 32, 0:128] = h
                spread[r:r + 32, 128:256] = l
            wcol = jnp.where(inside, w, 0.0)
            dy = suby - ro
            cover = cover + jnp.where(jnp.logical_and(dy >= 0.0, dy < float(TS)), wcol, 0.0)
            ros.append(ro)
        want = jnp.where(lanes < TS, ros[0], ros[1]) + lane_a
        pick[:, pair * 128:pair * 128 + 128] = jnp.where(suby == want, 1.0, 0.0).astype(BF)
    numer = jnp.dot(pick[...], spread[...], preferred_element_type=F32)
    coadd = (numer[:, :128] + numer[:, 128:]) / (1.0 + cover)

    edge_out[0] = coadd[0:8, :]
    edge_out[1] = coadd[120:128, :]
    lane8 = lax.broadcasted_iota(jnp.int32, (8, 128), 1)
    lcols = jnp.zeros((8, 128), F32)
    rcols = jnp.zeros((8, 128), F32)
    for k in range(16):
        blk = coadd[8 * k:8 * k + 8, :]
        here = jnp.logical_and(lane8 >= 8 * k, lane8 < 8 * k + 8)
        lcols = jnp.where(here, blk if k == 0 else pltpu.roll(blk, 8 * k, 1), lcols)
        rcols = jnp.where(here, blk if k == 15 else pltpu.roll(blk, 8 * k + 8, 1), rcols)
    edge_out[2] = lcols
    edge_out[3] = rcols
    plan = ((0, 1, (down, col)), (1, 0, (up, col)), (2, 3, (row, right)), (3, 2, (row, left)),
            (4, 1, (down, right)), (5, 1, (down, left)), (6, 0, (up, right)), (7, 0, (up, left)))
    copies = [pltpu.make_async_remote_copy(
        src_ref=edge_out.at[src], dst_ref=edge_in.at[slot], send_sem=esend_sem.at[slot],
        recv_sem=erecv_sem.at[slot], device_id=dev, device_id_type=MESH) for slot, src, dev in plan]
    for c in copies:
        c.start()
    p_ref[...] = jnp.zeros_like(p_ref)
    p_ref[7:135, 0:128] = coadd
    for c in copies:
        c.wait()

    has_up = jnp.where(row > 0, 1.0, 0.0)
    has_down = jnp.where(row < N_ROW - 1, 1.0, 0.0)
    has_left = jnp.where(col > 0, 1.0, 0.0)
    has_right = jnp.where(col < N_COL - 1, 1.0, 0.0)
    side = jnp.where(lane8 < TS, has_right, has_left)
    p_ref[0:7, 0:128] = edge_in[0][1:8, :] * has_up
    p_ref[135:142, 0:128] = edge_in[1][0:7, :] * has_down
    p_ref[0:7, 128:256] = (jnp.where(lane8 < TS, edge_in[5], edge_in[4]) * side * has_up)[1:8, :]
    p_ref[135:142, 128:256] = (jnp.where(lane8 < TS, edge_in[7], edge_in[6]) * side * has_down)[0:7, :]
    from_left = edge_in[2]
    from_right = edge_in[3]
    for k in range(16):
        r = from_right if k == 0 else pltpu.roll(from_right, 128 - 8 * k, 1)
        l = from_left if k == 15 else pltpu.roll(from_left, 120 - 8 * k, 1)
        p_ref[7 + 8 * k:15 + 8 * k, 128:256] = jnp.where(lane8 < TS, r, l) * side


def comm_call(*args):
    vm = pl.BlockSpec(memory_space=pltpu.VMEM)
    hbm = pl.BlockSpec(memory_space=pltpu.HBM)
    return pl.pallas_call(
        comm_kernel,
        out_shape=[jax.ShapeDtypeStruct((152, 256), F32)] + W_SHAPES,
        in_specs=[hbm] * 13,
        out_specs=[vm] * 5,
        scratch_shapes=[
            pltpu.SMEM((1, TILES_DEV), jnp.int32),
            pltpu.SMEM((1, TILES_DEV), jnp.int32),
            pltpu.SMEM((1, TILES_DEV), jnp.int32),
            pltpu.SMEM((1, TILES_DEV), F32),
            pltpu.VMEM((TILES_DEV, TS, TS), F32),
            pltpu.VMEM((TILES_DEV, TS, TS), F32),
            pltpu.VMEM((TILES_DEV, 3 * TS, TS), F32),
            pltpu.VMEM((9, 1, 32), F32),
            pltpu.VMEM((3, 1, 32), F32),
            pltpu.VMEM((9, 32, 32), F32),
            pltpu.VMEM((9, 32, 32), F32),
            pltpu.VMEM((TILES_DEV, 32, 128), F32),
            pltpu.VMEM((N_COL, 40, 128), F32),
            pltpu.VMEM((N_COL, 40, 128), F32),
            pltpu.VMEM((N_COL * TS, 256), BF),
            pltpu.VMEM((128, N_COL * TS), BF),
            pltpu.VMEM((4, 8, 128), F32),
            pltpu.VMEM((8, 8, 128), F32),
            pltpu.SemaphoreType.DMA((13,)),
            pltpu.SemaphoreType.DMA((N_COL,)),
            pltpu.SemaphoreType.DMA((N_COL,)),
            pltpu.SemaphoreType.DMA((8,)),
            pltpu.SemaphoreType.DMA((8,)),
        ],
        compiler_params=pltpu.CompilerParams(collective_id=0, has_side_effects=True, vmem_limit_bytes=32 << 20),
        name="coadd",
    )(*args)


def body(tiles, row_kernels, column_resample_kernels, destination, row_offset, col_offset, exposure_weight,
         first_filter, first_bias, second_filter, second_bias, third_filter, third_bias):
    line = lambda v: v.reshape(1, -1)
    taps = lambda f: jnp.transpose(f, (2, 3, 0, 1)).reshape(9, 32, 32)
    one = jnp.transpose(first_filter, (2, 3, 1, 0)).reshape(9, 1, 32)
    keep = lambda v: pltpu.with_memory_space_constraint(v, pltpu.HBM)
    p, w1, w2, w3, bias = comm_call(*map(keep, (
        destination.T, line(row_offset), line(col_offset), line(exposure_weight), tiles, row_kernels,
        column_resample_kernels, one, line(first_bias), taps(second_filter), line(second_bias),
        taps(third_filter), line(third_bias))))
    return conv_call(p, w1, w2, w3, bias)


def solution(mesh):
    held = P(("row", "col"))
    in_specs = (held,) * 7 + (P(),) * 6
    return jax.shard_map(body, mesh=mesh, in_specs=in_specs, out_specs=P(None, "row", "col"), check_vma=False)
```

```python
import functools
import jax
import jax.numpy as jnp
from jax import lax
from jax.experimental import pallas as pl
from jax.experimental.pallas import tpu as pltpu
from jax.sharding import PartitionSpec as P

BF = jnp.bfloat16
F32 = jnp.float32


def split(x):
    hi = x.astype(BF)
    return hi, (x - hi.astype(F32)).astype(BF)


def build_weights(f1_ref, vec_ref, f2_ref, f3_ref, w1_ref, w2_ref, w3_ref, bias_ref):
    for f_ref, w_ref in ((f2_ref, w2_ref), (f3_ref, w3_ref)):
        for dx in range(3):
            row = jnp.concatenate(
                [f_ref[dy * 3 + dx] for dy in range(3)] + [jnp.zeros((32, 160), F32)], axis=1)
            for yo in range(6):
                moved = row if yo == 0 else pltpu.roll(row, 32 * yo, 1)
                hi, lo = split(moved)
                w_ref[0, dx, yo * 32:(yo + 1) * 32, :] = hi
                w_ref[1, dx, yo * 32:(yo + 1) * 32, :] = lo
    rows = jnp.concatenate([f1_ref[k] for k in range(9)] + [vec_ref[k] for k in range(3)]
                           + [jnp.zeros((116, 32), F32)], axis=0)
    rows = jnp.concatenate([rows, jnp.zeros((128, 96), F32)], axis=1)
    turned = jnp.transpose(rows)[:32, :]
    hi, lo = split(turned)
    hi = hi.astype(F32)
    lo = lo.astype(F32)
    lane = lax.broadcasted_iota(jnp.int32, (32, 256), 1)
    base = jnp.where(lane == 144, hi[:, 9:10], 0.0) + jnp.where(lane == 145, lo[:, 9:10], 0.0)
    for yo in range(8):
        acc = base
        for part, w in enumerate((hi, hi, lo)):
            for dx in range(3):
                for dy in range(3):
                    k = dy * 3 + dx
                    acc = jnp.where(lane == part * 48 + dx * 16 + yo + dy, w[:, k:k + 1], acc)
        r = (yo % 2) * 128 + (yo // 2) * 32
        w1_ref[r:r + 32, :] = acc.astype(BF)
    for k in range(2):
        bias_ref[k] = jnp.broadcast_to(turned[:, 10 + k:11 + k], (32, 128))


def conv_body(row, col, p_ref, w1_ref, w2_ref, w3_ref, bias_ref, out_ref,
              ps, f_hi, f_lo, s_hi, s_lo, out_s, out_sem):
    p = p_ref[...]
    ps[0] = pltpu.roll(p, 1, 1)
    ps[1] = p
    ps[2] = pltpu.roll(p, 255, 1)
    lane = lax.broadcasted_iota(jnp.int32, (1, 256), 1)
    dead = jnp.logical_or(jnp.logical_and(col == 0, lane >= 192),
                          jnp.logical_and(col == 15, jnp.logical_and(lane >= 128, lane < 192)))
    cmask = jnp.where(dead, 0.0, 1.0)
    sub = lax.broadcasted_iota(jnp.int32, (16, 256), 0)
    ones = jnp.where(sub < 2, 1.0, 0.0).astype(BF)
    pad = jnp.zeros((96, 256), BF)
    w1 = w1_ref[...]
    n_rows = 1024
    base = row * 128

    def valid(y):
        if 0 <= y < 128:
            return 1.0
        yy = base + y
        return jnp.where(jnp.logical_and(yy >= 0, yy < n_rows), 1.0, 0.0)

    for g in range(18):
        hs, ls = [], []
        for dx in range(3):
            h, l = split(ps[dx, pl.ds(8 * g, 16), :])
            hs.append(h)
            ls.append(l)
        rhs = jnp.concatenate(hs + ls + hs + [ones, pad], axis=0)
        acc = jnp.dot(w1, rhs, preferred_element_type=F32)
        for q in range(2):
            for m in range(4):
                mask = cmask * valid(8 * g + 2 * m + q - 6)
                v = jnp.maximum(acc[q * 128 + m * 32:q * 128 + m * 32 + 32, :], 0.0) * mask
                h, l = split(v)
                at = pl.ds((4 * g + m) * 32, 32)
                f_hi[q, at, :] = h
                f_lo[q, at, :] = l

    b2 = jnp.concatenate([bias_ref[0], bias_ref[0]], axis=1)

    def second(hi, lo, places):
        parts = []
        for dx in range(3):
            parts.append(jnp.dot(w2_ref[0, dx], hi, preferred_element_type=F32)
                         + jnp.dot(w2_ref[1, dx], hi, preferred_element_type=F32)
                         + jnp.dot(w2_ref[0, dx], lo, preferred_element_type=F32))
        acc = parts[1] + pltpu.roll(parts[0], 2, 1) + pltpu.roll(parts[2], 254, 1)
        for yo, y, r, n in places:
            mask = cmask * valid(y)
            v = jnp.maximum(acc[yo * 32:yo * 32 + 32, :] + b2, 0.0) * mask
            at = pl.ds(n * 32, 32)
            for k, sh in enumerate((pltpu.roll(v, 4, 1), v, pltpu.roll(v, 252, 1))):
                h, l = split(sh[:, :128])
                s_hi[k, r, at, :] = h
                s_lo[k, r, at, :] = l

    for t in range(22):
        q = t % 2
        m0 = 6 * (t // 2)
        at = pl.ds(32 * m0, 256)
        second(f_hi[q, at, :], f_lo[q, at, :],
               [(yo, 2 * (m0 + yo) + q - 4, 2 * (yo % 2) + q, m0 // 2 + yo // 2) for yo in range(6)])

    tail = pl.ds(66 * 32, 128)
    both = lambda f: jnp.concatenate([f[0, tail, :], f[1, tail, :]], axis=0)
    second(both(f_hi), both(f_lo),
           [(4 * q + e, 2 * (66 + e) + q - 4, 2 * e + q, 33) for q in range(2) for e in range(2)])

    b3 = bias_ref[1]

    whole = out_s.reshape(32, 128, 128)
    writes = []
    def third(pick_block, places):
        hs, ls, wh, wl = [], [], [], []
        for dx in range(3):
            hs.append(pick_block(s_hi, dx))
            ls.append(pick_block(s_lo, dx))
            wh.append(w3_ref[0, dx])
            wl.append(w3_ref[1, dx])
        acc = jnp.dot(jnp.concatenate(wh + wl + wh, axis=1), jnp.concatenate(hs + hs + ls, axis=0),
                      preferred_element_type=F32)
        for yo, e, y in places:
            v = acc[yo * 32:yo * 32 + 32, e * 128:e * 128 + 128] + b3
            for k in range(4):
                out_s[pl.ds(k * 1024 + y, 8, stride=128), :] = v[8 * k:8 * k + 8, :]

    for step in range(6):
        first, count = 24 * step, 24
        if step < 5:
            at = pl.ds(32 * 6 * step, 256)
            for half in range(2):
                third(lambda s, dx: jnp.concatenate([s[dx, 2 * half, at, :], s[dx, 2 * half + 1, at, :]], axis=1),
                      [(yo, e, 4 * (6 * step + yo) + 2 * half + e) for e in range(2) for yo in range(6)])
        else:
            count = 8
            at = pl.ds(32 * 30, 128)
            third(lambda s, dx: jnp.concatenate(
                [jnp.concatenate([s[dx, 2 * half, at, :], s[dx, 2 * half + 1, at, :]], axis=1) for half in range(2)],
                axis=0),
                [(4 * half + f, e, 4 * (30 + f) + 2 * half + e)
                 for half in range(2) for e in range(2) for f in range(2)])
        rows = pl.ds(first, count)
        writes.append(pltpu.make_async_copy(whole.at[:, rows, :], out_ref.at[:, rows, :], out_sem.at[step]))
        writes[-1].start()
    for w in writes:
        w.wait()


def conv_kernel(*refs):
    conv_body(lax.axis_index("row"), lax.axis_index("col"), *refs)


W_SHAPES = [jax.ShapeDtypeStruct((256, 256), BF), jax.ShapeDtypeStruct((2, 3, 192, 256), BF),
            jax.ShapeDtypeStruct((2, 3, 192, 256), BF), jax.ShapeDtypeStruct((2, 32, 128), F32)]


def conv_call(p, w1, w2, w3, bias):
    vm = pl.BlockSpec(memory_space=pltpu.VMEM)
    return pl.pallas_call(
        conv_kernel,
        out_shape=jax.ShapeDtypeStruct((32, 128, 128), F32),
        in_specs=[vm] * 5,
        out_specs=pl.BlockSpec(memory_space=pltpu.HBM),
        scratch_shapes=[pltpu.VMEM((3, 152, 256), F32),
                        pltpu.VMEM((2, 74 * 32, 256), BF), pltpu.VMEM((2, 74 * 32, 256), BF),
                        pltpu.VMEM((3, 4, 34 * 32, 128), BF), pltpu.VMEM((3, 4, 34 * 32, 128), BF),
                        pltpu.VMEM((4096, 128), F32), pltpu.SemaphoreType.DMA((6,))],
        compiler_params=pltpu.CompilerParams(vmem_limit_bytes=48 << 20),
        name="convs",
    )(p, w1, w2, w3, bias)


N_ROW = 8
N_COL = 16
TILES_DEV = 8
TS = 64
MESH = pl.DeviceIdType.MESH
ORDER = (10, 1, 4, 3, 12, 2, 8, 5, 15, 7, 13, 6, 9, 14, 11)


def dot3(ah, al, bh, bl, dims):
    d = functools.partial(lax.dot_general, dimension_numbers=(dims, ((), ())), preferred_element_type=F32)
    return d(ah, bh) + d(al, bh) + d(ah, bl)


def comm_kernel(dest_h, roff_h, coff_h, wgt_h, tiles_h, rker_h, cker_h, f1_h, b1_h, f2_h, b2_h, f3_h, b3_h,
                p_ref, w1_ref, w2_ref, w3_ref, bias_ref,
                dest, roff, coff, wgt, tiles, rker, ckpad, f1, vec, f2, f3, packed, send, recv, spread, pick,
                edge_out, edge_in, in_sem, send_sem, recv_sem, esend_sem, erecv_sem):
    half = TILES_DEV // 2
    pairs = []
    for h in range(2):
        part = pl.ds(h * half, half)
        pairs += [(rker_h.at[part], rker.at[part]), (tiles_h.at[part], tiles.at[part])]
        if h == 0:
            pairs += [(cker_h, ckpad.at[:, pl.ds(TS, TS), :]), (coff_h, coff)]
    pairs += [(dest_h, dest), (roff_h, roff), (wgt_h, wgt), (f2_h, f2), (f3_h, f3),
              (f1_h, f1), (b1_h, vec.at[0]), (b2_h, vec.at[1]), (b3_h, vec.at[2])]
    fetches = [pltpu.make_async_copy(src, dst, in_sem.at[i]) for i, (src, dst) in enumerate(pairs)]
    for f in fetches[:9]:
        f.start()
    row = lax.axis_index("row")
    col = lax.axis_index("col")
    up = lax.rem(row + N_ROW - 1, N_ROW)
    down = lax.rem(row + 1, N_ROW)
    left = lax.rem(col + N_COL - 1, N_COL)
    right = lax.rem(col + 1, N_COL)

    barrier = pltpu.get_barrier_semaphore()

    @pl.loop(1, N_COL)
    def _(k):
        pl.semaphore_signal(barrier, inc=1, device_id=(row, lax.rem(col + k, N_COL)), device_id_type=MESH)

    for r in (up, down):
        for c in (left, col, right):
            pl.semaphore_signal(barrier, inc=1, device_id=(r, c), device_id_type=MESH)

    for f in fetches[9:]:
        f.start()
    blank = jnp.zeros((TILES_DEV, TS, TS), F32)
    ckpad[:, 0:TS, :] = blank
    ckpad[:, 2 * TS:3 * TS, :] = blank
    for t in range(TILES_DEV):
        if t % half == 0:
            for f in fetches[:4] if t == 0 else fetches[4:6]:
                f.wait()
        rh, rl = split(rker[t])
        th, tl = split(tiles[t])
        mid = dot3(rh, rl, th, tl, ((1,), (0,)))
        placed = ckpad[t, pl.ds(TS - coff[0, t], 2 * TS), :]
        mh, ml = split(mid)
        ch, cl = split(placed)
        img = dot3(mh, ml, ch, cl, ((1,), (1,)))
        packed[t] = img[:32, :] + pltpu.roll(img[32:, :], 64, 1)
    for f in fetches[6:9]:
        f.wait()

    sub8 = lax.broadcasted_iota(jnp.int32, (8, 128), 0)

    @pl.loop(0, N_COL, unroll=4)
    def _(c):
        acc = None
        ro = jnp.float32(0.0)
        co = jnp.float32(0.0)
        w = jnp.float32(0.0)
        for t in range(TILES_DEV):
            hit = jnp.where(dest[0, t] == c, 1.0, 0.0)
            wt = hit * wgt[0, t]
            ro = ro + hit * roff[0, t].astype(F32)
            co = co + hit * coff[0, t].astype(F32)
            w = w + wt
            term = packed[t] * wt
            acc = term if acc is None else acc + term
        send[c, 0:32, :] = acc
        send[c, 32:40, :] = jnp.where(sub8 == 0, ro, jnp.where(sub8 == 1, co, w))

    pl.semaphore_wait(barrier, N_COL - 1 + 6)

    def tile_copy(k):
        c = lax.rem(col + k, N_COL)
        return pltpu.make_async_remote_copy(
            src_ref=send.at[c], dst_ref=recv.at[k], send_sem=send_sem.at[k], recv_sem=recv_sem.at[k],
            device_id=(row, c), device_id_type=MESH)

    for k in ORDER:
        tile_copy(k).start()

    recv[0] = send[col]
    for f in fetches[9:]:
        f.wait()
    build_weights(f1, vec, f2, f3, w1_ref, w2_ref, w3_ref, bias_ref)

    lane = lax.broadcasted_iota(jnp.int32, (1, 128), 1).astype(F32)
    suby = lax.broadcasted_iota(jnp.int32, (128, 128), 0).astype(F32)
    lanes = lax.broadcasted_iota(jnp.int32, (128, 128), 1)
    lane_a = (lanes % TS).astype(F32)
    cover = jnp.zeros((128, 128), F32)
    for pair in range(N_COL // 2):
        ros = []
        for e in range(2):
            s = 2 * pair + e
            if s > 0:
                tile_copy(ORDER[s - 1]).wait()
            at = ORDER[s - 1] if s > 0 else 0
            pk = recv[at, 0:32, :]
            ro = recv[at, 32:33, :]
            co = recv[at, 33:34, :]
            w = recv[at, 34:35, :]
            off = lane - co
            inside = jnp.logical_and(off >= 0.0, off < float(TS))
            a = jnp.where(inside, pk, 0.0)
            b = jnp.where(inside, pltpu.roll(pk, 64, 1), 0.0)
            for half, v in enumerate((a, b)):
                h, l = split(v)
                r = s * TS + half * 32
                spread[r:r + 32, 0:128] = h
                spread[r:r + 32, 128:256] = l
            wcol = jnp.where(inside, w, 0.0)
            dy = suby - ro
            cover = cover + jnp.where(jnp.logical_and(dy >= 0.0, dy < float(TS)), wcol, 0.0)
            ros.append(ro)
        want = jnp.where(lanes < TS, ros[0], ros[1]) + lane_a
        pick[:, pair * 128:pair * 128 + 128] = jnp.where(suby == want, 1.0, 0.0).astype(BF)
    numer = jnp.dot(pick[...], spread[...], preferred_element_type=F32)
    coadd = (numer[:, :128] + numer[:, 128:]) / (1.0 + cover)

    edge_out[0] = coadd[0:8, :]
    edge_out[1] = coadd[120:128, :]
    lane8 = lax.broadcasted_iota(jnp.int32, (8, 128), 1)
    lcols = jnp.zeros((8, 128), F32)
    rcols = jnp.zeros((8, 128), F32)
    for k in range(16):
        blk = coadd[8 * k:8 * k + 8, :]
        here = jnp.logical_and(lane8 >= 8 * k, lane8 < 8 * k + 8)
        lcols = jnp.where(here, blk if k == 0 else pltpu.roll(blk, 8 * k, 1), lcols)
        rcols = jnp.where(here, blk if k == 15 else pltpu.roll(blk, 8 * k + 8, 1), rcols)
    edge_out[2] = lcols
    edge_out[3] = rcols
    plan = ((0, 1, (down, col)), (1, 0, (up, col)), (2, 3, (row, right)), (3, 2, (row, left)),
            (4, 1, (down, right)), (5, 1, (down, left)), (6, 0, (up, right)), (7, 0, (up, left)))
    copies = [pltpu.make_async_remote_copy(
        src_ref=edge_out.at[src], dst_ref=edge_in.at[slot], send_sem=esend_sem.at[slot],
        recv_sem=erecv_sem.at[slot], device_id=dev, device_id_type=MESH) for slot, src, dev in plan]
    for c in copies:
        c.start()
    p_ref[...] = jnp.zeros_like(p_ref)
    p_ref[7:135, 0:128] = coadd
    for c in copies:
        c.wait()

    has_up = jnp.where(row > 0, 1.0, 0.0)
    has_down = jnp.where(row < N_ROW - 1, 1.0, 0.0)
    has_left = jnp.where(col > 0, 1.0, 0.0)
    has_right = jnp.where(col < N_COL - 1, 1.0, 0.0)
    side = jnp.where(lane8 < TS, has_right, has_left)
    p_ref[0:7, 0:128] = edge_in[0][1:8, :] * has_up
    p_ref[135:142, 0:128] = edge_in[1][0:7, :] * has_down
    p_ref[0:7, 128:256] = (jnp.where(lane8 < TS, edge_in[5], edge_in[4]) * side * has_up)[1:8, :]
    p_ref[135:142, 128:256] = (jnp.where(lane8 < TS, edge_in[7], edge_in[6]) * side * has_down)[0:7, :]
    from_left = edge_in[2]
    from_right = edge_in[3]
    for k in range(16):
        r = from_right if k == 0 else pltpu.roll(from_right, 128 - 8 * k, 1)
        l = from_left if k == 15 else pltpu.roll(from_left, 120 - 8 * k, 1)
        p_ref[7 + 8 * k:15 + 8 * k, 128:256] = jnp.where(lane8 < TS, r, l) * side


def comm_call(*args):
    vm = pl.BlockSpec(memory_space=pltpu.VMEM)
    hbm = pl.BlockSpec(memory_space=pltpu.HBM)
    return pl.pallas_call(
        comm_kernel,
        out_shape=[jax.ShapeDtypeStruct((152, 256), F32)] + W_SHAPES,
        in_specs=[hbm] * 13,
        out_specs=[vm] * 5,
        scratch_shapes=[
            pltpu.SMEM((1, TILES_DEV), jnp.int32),
            pltpu.SMEM((1, TILES_DEV), jnp.int32),
            pltpu.SMEM((1, TILES_DEV), jnp.int32),
            pltpu.SMEM((1, TILES_DEV), F32),
            pltpu.VMEM((TILES_DEV, TS, TS), F32),
            pltpu.VMEM((TILES_DEV, TS, TS), F32),
            pltpu.VMEM((TILES_DEV, 3 * TS, TS), F32),
            pltpu.VMEM((9, 1, 32), F32),
            pltpu.VMEM((3, 1, 32), F32),
            pltpu.VMEM((9, 32, 32), F32),
            pltpu.VMEM((9, 32, 32), F32),
            pltpu.VMEM((TILES_DEV, 32, 128), F32),
            pltpu.VMEM((N_COL, 40, 128), F32),
            pltpu.VMEM((N_COL, 40, 128), F32),
            pltpu.VMEM((N_COL * TS, 256), BF),
            pltpu.VMEM((128, N_COL * TS), BF),
            pltpu.VMEM((4, 8, 128), F32),
            pltpu.VMEM((8, 8, 128), F32),
            pltpu.SemaphoreType.DMA((15,)),
            pltpu.SemaphoreType.DMA((N_COL,)),
            pltpu.SemaphoreType.DMA((N_COL,)),
            pltpu.SemaphoreType.DMA((8,)),
            pltpu.SemaphoreType.DMA((8,)),
        ],
        compiler_params=pltpu.CompilerParams(collective_id=0, has_side_effects=True, vmem_limit_bytes=32 << 20),
        name="coadd",
    )(*args)


def body(tiles, row_kernels, column_resample_kernels, destination, row_offset, col_offset, exposure_weight,
         first_filter, first_bias, second_filter, second_bias, third_filter, third_bias):
    line = lambda v: v.reshape(1, -1)
    taps = lambda f: jnp.transpose(f, (2, 3, 0, 1)).reshape(9, 32, 32)
    one = jnp.transpose(first_filter, (2, 3, 1, 0)).reshape(9, 1, 32)
    keep = lambda v: pltpu.with_memory_space_constraint(v, pltpu.HBM)
    p, w1, w2, w3, bias = comm_call(*map(keep, (
        destination.T, line(row_offset), line(col_offset), line(exposure_weight), tiles, row_kernels,
        column_resample_kernels, one, line(first_bias), taps(second_filter), line(second_bias),
        taps(third_filter), line(third_bias))))
    return conv_call(p, w1, w2, w3, bias)


def solution(mesh):
    held = P(("row", "col"))
    in_specs = (held,) * 7 + (P(),) * 6
    return jax.shard_map(body, mesh=mesh, in_specs=in_specs, out_specs=P(None, "row", "col"), check_vma=False)
```
